32 devices in a mesh: bx: 8 (over z, x), by: 4 (over y, core).
Axes of the slice: x: 2, y: 2, z: 4, core: 2. Of those that a mesh axis runs over, the one named last changes fastest.
Arguments:
- tokens: bfloat16 [8, 4, 1024, 512], P('bx', 'by'), may hold values from -6 to 6
- norm_gain: float32 [512], replicated, may hold values from 0.1 to 1.9
- w_query_key: bfloat16 [512, 1024], replicated
- w_value: bfloat16 [512, 512], replicated, may hold values from -1 to 1
- w_out: bfloat16 [512, 512], replicated, may hold values from -0.25 to 0.25
- cotangent: bfloat16 [8, 4, 1024, 512], P('bx', 'by'), may hold values from -6 to 6
- block_order: int32 [8, 4, 1024], P('bx', 'by'), may hold values from 0 to 1023, each once within a row
- neighbour_ids: int32 [8, 4, 4, 4], replicated, may hold values from 0 to 127, as said below
- neighbour_count: int32 [8, 4, 4], replicated, may hold values from 1 to 4
Outputs:
- branch_out: bfloat16 [8, 4, 1024, 512], P('bx', 'by')
- grad_tokens: float32 [8, 4, 1024, 512], P('bx', 'by')
- grad_w_query_key: float32 [512, 1024], replicated
- grad_w_value: float32 [512, 512], replicated
- grad_w_out: float32 [512, 512], replicated
- grad_norm_gain: float32 [512], replicated
The draws below stay inside these ranges and needn't reach their ends.
Inputs may be any that keep to these rules, and one draw needn't show every extreme that they name: `neighbour_ids`: block ids are (x * 4 + y) * 4 + b. Entry j < neighbour_count of query block b on brick (x, y) names a block other than b itself, either another block of brick (x, y) or a block of a brick one step away along exactly one axis (x - 1, x + 1, y - 1 or y + 1); the live entries of one list differ. Entries from neighbour_count on hold the query block's own id. Over all query blocks of one brick, at most 2 distinct blocks of any one other brick are named, and every brick names exactly 2 blocks of some other brick. `block_order`: on every brick, a permutation of the arrival rows.
All inputs are finite; a program needn't handle non-finite values.
Results may differ from the reference program's by a relative error of at most 0.006.
The reference program's roundings to bfloat16 on the way count: a program that leaves them out, or rounds other values in their place, can miss the bound.
Values may be sent and summed in bfloat16 or wider, within the bound.
A program may use at most 256 MiB of HBM per device.

```python
import math
import jax
import jax.numpy as jnp
from jax import lax

D = 512
HEADS = 8
BLK = 256
NB = 4
CAP = 2
BLK_DEV = 4
TOK_DEV = 1024
BRICKS_X = 8
BRICKS_Y = 4


def neighbour_tables(key):
    base_key = jax.random.fold_in(key, 7)
    key_offer, key_score, key_first, key_second = jax.random.split(base_key, 4)
    grid_x = jnp.arange(BRICKS_X, dtype=jnp.int32)[:, None, None]
    grid_y = jnp.arange(BRICKS_Y, dtype=jnp.int32)[None, :, None]
    step_x = jnp.array([-1, 1, 0, 0], dtype=jnp.int32)
    step_y = jnp.array([0, 0, -1, 1], dtype=jnp.int32)
    near_x, near_y = jnp.broadcast_arrays(grid_x + step_x, grid_y + step_y)
    inside = (near_x >= 0) & (near_x < BRICKS_X) & (near_y >= 0) & (near_y < BRICKS_Y)
    near_brick = jnp.clip(near_x, 0, BRICKS_X - 1) * BRICKS_Y + jnp.clip(near_y, 0, BRICKS_Y - 1)
    block_range = jnp.arange(BLK_DEV, dtype=jnp.int32)
    offer_scores = jax.random.randint(key_offer, (BRICKS_X, BRICKS_Y, 4, BLK_DEV), 0, 1 << 20) * BLK_DEV + block_range
    offered = jnp.argsort(offer_scores, axis=-1, stable=True)[..., :CAP].astype(jnp.int32)
    offer_ids = (near_brick[..., None] * BLK_DEV + offered).reshape(BRICKS_X, BRICKS_Y, 4 * CAP)
    offer_fine = jnp.repeat(inside, CAP, axis=-1)
    own_brick = grid_x[..., 0] * BRICKS_Y + grid_y[..., 0]
    own_ids = own_brick[..., None] * BLK_DEV + block_range
    columns = BLK_DEV + 4 * CAP
    candidates = jnp.concatenate([jnp.broadcast_to(own_ids[:, :, None, :], (BRICKS_X, BRICKS_Y, BLK_DEV, BLK_DEV)), jnp.broadcast_to(offer_ids[:, :, None, :], (BRICKS_X, BRICKS_Y, BLK_DEV, 4 * CAP))], axis=-1)
    candidate_fine = jnp.concatenate([jnp.broadcast_to(block_range[:, None] != block_range[None, :], (BRICKS_X, BRICKS_Y, BLK_DEV, BLK_DEV)), jnp.broadcast_to(offer_fine[:, :, None, :], (BRICKS_X, BRICKS_Y, BLK_DEV, 4 * CAP))], axis=-1)
    column_range = jnp.arange(columns, dtype=jnp.int32)
    scores = jax.random.randint(key_score, (BRICKS_X, BRICKS_Y, BLK_DEV, columns), 0, 1 << 20) * columns + column_range
    forced_dir = jnp.where(jnp.arange(BRICKS_X, dtype=jnp.int32) < BRICKS_X - 1, 1, 0)[:, None, None, None]
    forced = (block_range[:, None] == 0) & (column_range >= BLK_DEV) & ((column_range - BLK_DEV) // CAP == forced_dir)
    scores = jnp.where(forced, scores + (1 << 26), scores)
    scores = jnp.where(candidate_fine, scores, -1 - column_range)
    _, picked = lax.top_k(scores, NB)
    chosen = jnp.take_along_axis(candidates, picked, axis=-1)
    first_count = jax.random.randint(key_first, (BRICKS_X, BRICKS_Y, BLK_DEV), 1, NB + 1)
    second_count = jax.random.randint(key_second, (BRICKS_X, BRICKS_Y, BLK_DEV), 1, NB + 1)
    counts = jnp.maximum(first_count, second_count)
    counts = jnp.where(block_range == 0, NB, jnp.where(block_range == BLK_DEV - 1, 1, counts))
    listed = jnp.where(jnp.arange(NB, dtype=jnp.int32) < counts[..., None], chosen, own_ids[..., None])
    return (listed.astype(jnp.int32), counts.astype(jnp.int32))


def draw_neighbour_ids(key, part):
    listed, _ = neighbour_tables(key)
    return listed


def draw_neighbour_count(key, part):
    _, counts = neighbour_tables(key)
    return counts


def draw_tokens(key, part):
    row_shape = (BRICKS_X, BRICKS_Y, TOK_DEV, D)
    key_base = jax.random.fold_in(jax.random.fold_in(key, 5), 0)
    key_scale = jax.random.fold_in(jax.random.fold_in(key, 5), 2)
    row_scale = jnp.exp(jax.random.uniform(key_scale, (BRICKS_X, BRICKS_Y, TOK_DEV, 1), jnp.float32, -1.0, 1.0))
    token_rows = jax.random.normal(key_base, row_shape, jnp.float32) * row_scale
    return jnp.clip(token_rows, -6.0, 6.0).astype(jnp.bfloat16)


def draw_w_query_key(key, part):
    key_query, key_key = jax.random.split(jax.random.fold_in(key, 11), 2)
    spread = D ** (-0.5)
    w_query = jax.random.normal(key_query, (D, D), jnp.float32) * spread
    w_key = jax.random.normal(key_key, (D, D), jnp.float32) * spread
    return jnp.concatenate([w_query, w_key], axis=1).astype(jnp.bfloat16)


def shard_levels(key, shape, cuts, least, largest):
    def one(dim, shards_of):
        steps = jax.random.uniform(jax.random.fold_in(jax.random.fold_in(key, 6), dim), (shards_of,), jnp.float32, least / len(cuts), largest / len(cuts))
        return jnp.repeat(jnp.exp(steps), shape[dim] // shards_of).reshape((-1,) + (1,) * (len(shape) - dim - 1))

    gain = one(*cuts[0])
    for cut in cuts[1:]:
        gain = gain * one(*cut)
    return gain


def noise(rng, dims, scale, bound, pieces=(), held_as=jnp.bfloat16):
    gain = shard_levels(rng, dims, pieces, -0.22, 0.18) if pieces else 1.0
    values = jax.random.normal(rng, dims, jnp.float32) * scale * gain
    return jnp.minimum(jnp.maximum(values, -bound), bound).astype(held_as)


def setup_inputs(seed: int = 0) -> dict:
    arg_keys = jax.random.split(jax.random.key(seed), 10)
    tokens = draw_tokens(jax.random.fold_in(arg_keys[9], 71), 0)
    norm_gain = jnp.clip(1.0 + 0.18 * jax.random.normal(arg_keys[1], (D,), jnp.float32), 0.1, 1.9)
    w_query_key = draw_w_query_key(jax.random.fold_in(arg_keys[9], 71), 0)
    w_value = noise(arg_keys[3], (D, D), (D // 16) ** -0.5, 1.0)
    w_out = noise(arg_keys[4], (D, D), D ** -0.5, 0.25)
    cotangent = noise(arg_keys[5], (BRICKS_X, BRICKS_Y, TOK_DEV, D), 1.0, 6.0, ((0, 8), (1, 4)))
    block_order = jax.vmap(lambda own: jax.random.permutation(own, TOK_DEV))(jax.random.split(arg_keys[6], BRICKS_X * BRICKS_Y)).reshape((BRICKS_X, BRICKS_Y, TOK_DEV)).astype(jnp.int32)
    neighbour_ids = draw_neighbour_ids(jax.random.fold_in(arg_keys[9], 71), 0)
    neighbour_count = draw_neighbour_count(jax.random.fold_in(arg_keys[9], 71), 0)
    return dict(tokens=tokens, norm_gain=norm_gain, w_query_key=w_query_key, w_value=w_value, w_out=w_out, cotangent=cotangent, block_order=block_order, neighbour_ids=neighbour_ids, neighbour_count=neighbour_count)


EPSILON = 1e-06

def rms_rows(token_rows, gain_row):
    values = token_rows.astype(jnp.float32)
    inv_rms = lax.rsqrt(lax.optimization_barrier(jnp.mean(values * values, axis=-1, keepdims=True)) + EPSILON)
    return (values, inv_rms, (values * inv_rms * gain_row).astype(jnp.bfloat16))

def attend_block(query_rows, key_value_rows, live_cols, grad_context):
    features = query_rows.shape[-1]
    head_size = features // HEADS
    row_count = query_rows.shape[0]
    factor = 1.0 / math.sqrt(head_size)
    highest = lax.Precision.HIGHEST
    queries = query_rows.reshape(row_count, HEADS, head_size).astype(jnp.float32)
    kv_rows = key_value_rows.reshape(-1, 2 * features)
    key_rows = kv_rows[:, :features].reshape(-1, HEADS, head_size).astype(jnp.float32)
    value_rows = kv_rows[:, features:].reshape(-1, HEADS, head_size).astype(jnp.float32)
    grad_rows = grad_context.reshape(row_count, HEADS, head_size).astype(jnp.float32)
    scores = jnp.einsum('ihd,jhd->hij', queries, key_rows, precision=highest) * factor
    scores = jnp.where(live_cols[None, None, :], scores, -1e+30)
    row_max = lax.optimization_barrier(jnp.max(scores, axis=-1, keepdims=True))
    powers = jnp.exp(scores - row_max)
    attn_probs = powers / lax.optimization_barrier(jnp.sum(powers, axis=-1, keepdims=True))
    probs_low = attn_probs.astype(jnp.bfloat16)
    context = jnp.einsum('hij,jhd->ihd', probs_low.astype(jnp.float32), value_rows, precision=highest).astype(jnp.bfloat16)
    grad_probs = jnp.einsum('ihd,jhd->hij', grad_rows, value_rows, precision=highest)
    centre = lax.optimization_barrier(jnp.sum(attn_probs * grad_probs, axis=-1, keepdims=True))
    grad_scores = (attn_probs * (grad_probs - centre) * factor).astype(jnp.bfloat16)
    grad_query = jnp.einsum('hij,jhd->ihd', grad_scores.astype(jnp.float32), key_rows, precision=highest).astype(jnp.bfloat16)
    grad_keys = jnp.einsum('hij,ihd->jhd', grad_scores.astype(jnp.float32), queries, precision=highest)
    grad_values = jnp.einsum('hij,ihd->jhd', probs_low.astype(jnp.float32), grad_rows, precision=highest)
    slots = key_value_rows.shape[0]
    return (context.reshape(row_count, features), grad_query.reshape(row_count, features), grad_keys.reshape(slots, row_count, features), grad_values.reshape(slots, row_count, features))

def reference(tokens, norm_gain, w_query_key, w_value, w_out, cotangent, block_order, neighbour_ids, neighbour_count):
    bricks = BRICKS_X * BRICKS_Y
    features = D
    row_order = block_order.reshape(bricks, TOK_DEV)
    sorted_rows = jnp.take_along_axis(tokens.reshape(bricks, TOK_DEV, features), row_order[:, :, None], axis=1).reshape(-1, features)
    sorted_grad = jnp.take_along_axis(cotangent.reshape(bricks, TOK_DEV, features), row_order[:, :, None], axis=1).reshape(-1, features)
    values, inv_rms, normed = rms_rows(sorted_rows, norm_gain)
    query_rows = jnp.dot(normed, w_query_key[:, :features], preferred_element_type=jnp.float32).astype(jnp.bfloat16)
    w_pair = jnp.concatenate([w_query_key[:, features:], w_value], axis=1)
    key_value = jnp.dot(normed, w_pair, preferred_element_type=jnp.float32).astype(jnp.bfloat16)
    key_value = key_value.reshape(bricks * BLK_DEV, BLK, 2 * features)
    d_context = jnp.dot(sorted_grad, w_out.T, preferred_element_type=jnp.float32).astype(jnp.bfloat16)
    all_ids = neighbour_ids.reshape(bricks, BLK_DEV, NB)
    all_counts = neighbour_count.reshape(bricks, BLK_DEV)
    query_blocks = query_rows.reshape(bricks, BLK_DEV, BLK, features)
    grad_blocks = d_context.reshape(bricks, BLK_DEV, BLK, features)
    entries = BLK_DEV * (NB + 1)

    def per_block(block_item):
        block_query, block_grad, key_ids, live_slots = block_item
        live_cols = jnp.repeat(live_slots, BLK)
        return attend_block(block_query, key_value[key_ids], live_cols, block_grad)

    def per_brick(grad_total, brick_item):
        brick, brick_query, brick_grad, brick_ids, brick_count = brick_item
        own_ids = brick * BLK_DEV + jnp.arange(BLK_DEV, dtype=jnp.int32)
        key_ids = jnp.concatenate([own_ids[:, None], brick_ids.astype(jnp.int32)], axis=1)
        live_slots = jnp.concatenate([jnp.ones((BLK_DEV, 1), dtype=jnp.bool_), jnp.arange(NB, dtype=jnp.int32)[None, :] < brick_count[:, None]], axis=1)
        context, grad_query, key_terms, value_terms = lax.map(per_block, (brick_query, brick_grad, key_ids, live_slots))
        flat_ids = key_ids.reshape(entries)
        flat_terms = jnp.concatenate([key_terms, value_terms], axis=-1).reshape(entries, BLK * 2 * features)
        same_block = (flat_ids[:, None] == flat_ids[None, :]).astype(jnp.float32)
        summed = jnp.dot(same_block, flat_terms, precision=lax.Precision.HIGHEST)
        earlier = lax.optimization_barrier(jnp.sum(jnp.tril(same_block, -1), axis=1))
        owned = flat_ids // BLK_DEV == brick
        shipped = lax.optimization_barrier(summed.astype(jnp.bfloat16)).astype(jnp.float32)
        partial_sums = jnp.where(owned[:, None], summed, shipped)
        partial_sums = jnp.where((earlier == 0)[:, None], partial_sums, jnp.zeros_like(partial_sums))
        grad_total = grad_total.at[flat_ids].add(partial_sums.reshape(entries, BLK, 2 * features))
        return (grad_total, (context, grad_query))
    start_total = jnp.zeros((bricks * BLK_DEV, BLK, 2 * features), jnp.float32)
    grad_total, (context, grad_query) = lax.scan(per_brick, start_total, (jnp.arange(bricks, dtype=jnp.int32), query_blocks, grad_blocks, all_ids, all_counts))
    grad_kv = grad_total.astype(jnp.bfloat16).reshape(-1, 2 * features)
    context = context.reshape(-1, features)
    grad_query = grad_query.reshape(-1, features)
    out_rows = jnp.dot(context, w_out, preferred_element_type=jnp.float32).astype(jnp.bfloat16)
    grad_w_out = jnp.dot(context.T, sorted_grad, preferred_element_type=jnp.float32)
    grad_proj = jnp.concatenate([grad_query, grad_kv], axis=1)
    w_all = jnp.concatenate([w_query_key, w_value], axis=1)
    grad_normed = jnp.dot(grad_proj, w_all.T, preferred_element_type=jnp.float32)
    grad_all = jnp.dot(normed.T, grad_proj, preferred_element_type=jnp.float32)
    grad_norm_gain = lax.optimization_barrier(jnp.sum(grad_normed * (values * inv_rms), axis=0))
    scaled_grad = grad_normed * norm_gain
    grad_rows = inv_rms * scaled_grad - values * (inv_rms * inv_rms * inv_rms) * lax.optimization_barrier(jnp.mean(values * scaled_grad, axis=-1, keepdims=True))
    inverse = jnp.argsort(row_order, axis=1).astype(jnp.int32)
    branch_out = jnp.take_along_axis(out_rows.reshape(bricks, TOK_DEV, features), inverse[:, :, None], axis=1)
    grad_tokens = jnp.take_along_axis(grad_rows.reshape(bricks, TOK_DEV, features), inverse[:, :, None], axis=1)
    return (branch_out.reshape(BRICKS_X, BRICKS_Y, TOK_DEV, features), grad_tokens.reshape(BRICKS_X, BRICKS_Y, TOK_DEV, features), grad_all[:, :2 * features], grad_all[:, 2 * features:], grad_w_out, grad_norm_gain)
```

```python
import functools
import math

import jax
import jax.numpy as jnp
from jax import lax
from jax.experimental import pallas as pl
from jax.experimental.pallas import tpu as pltpu
from jax.sharding import PartitionSpec as P

HEADS = 8
BLK = 256
CAP = 2
LANES = 128
CHUNKS = 4
PIECES = 8
FIRST_PIECES = 1
PACE = 1
EPSILON = 1e-06
MESH = pl.DeviceIdType.MESH
SIDES = ((-1, 0), (1, 0), (0, -1), (0, 1))


def dot(a, b):
    return jnp.dot(a, b, preferred_element_type=jnp.float32)


def dot_nt(a, b):
    return lax.dot_general(a, b, (((1,), (1,)), ((), ())), preferred_element_type=jnp.float32)


def dot_tn(a, b):
    return lax.dot_general(a, b, (((0,), (0,)), ((), ())), preferred_element_type=jnp.float32)


def low(a):
    return a.astype(jnp.bfloat16)


def sides_of(x, y, extents):
    found = []
    for step_x, step_y in SIDES:
        to_x, to_y = x + step_x, y + step_y
        inside = (to_x >= 0) & (to_x < extents[0]) & (to_y >= 0) & (to_y < extents[1])
        found.append(
            (inside, jnp.clip(to_x, 0, extents[0] - 1), jnp.clip(to_y, 0, extents[1] - 1))
        )
    return found


def peers_of(sides):
    return sum(jnp.where(inside, 1, 0) for inside, _, _ in sides)


def wanted_blocks(ids, counts, x, y, inside, first_id, blocks):
    bits = [jnp.int32(0)] * blocks
    for b in range(blocks):
        live = counts[y, b, x]
        for j in range(ids.shape[2]):
            offset = ids[y, b, j, x] - first_id
            hit = inside & (j < live)
            bits = [jnp.where(hit & (offset == o), 1, bits[o]) for o in range(blocks)]
    return bits


def ranks_of(bits):
    ranks, count = [], jnp.int32(0)
    for bit in bits:
        ranks.append(count)
        count = count + bit
    return ranks


def fetch_kernel(
    ids,
    counts,
    order_ref,
    tokens_ref,
    cotangent_ref,
    gain_ref,
    w_qk_ref,
    w_value_ref,
    w_out_ref,
    table_ref,
    sorted_ref,
    cot_ref,
    normed_ref,
    q_ref,
    g_ref,
    kv_ref,
    send,
    recv,
    send_sem,
    recv_sem,
    *,
    extents,
):
    x, y = lax.axis_index("bx"), lax.axis_index("by")
    sides = sides_of(x, y, extents)
    blocks, blk, features = sorted_ref.shape
    rows = blocks * blk
    slots = ids.shape[2]

    barrier = pltpu.get_barrier_semaphore()
    for inside, to_x, to_y in sides:

        @pl.when(inside)
        def _():
            pl.semaphore_signal(barrier, inc=1, device_id=(to_x, to_y), device_id_type=MESH)

    order = jnp.broadcast_to(order_ref[...].astype(jnp.float32), (LANES, rows)).T
    lane = lax.broadcasted_iota(jnp.int32, (rows, LANES), 1).astype(jnp.float32)
    order_mask = jnp.concatenate(
        [low(jnp.where(order == lane + t * LANES, 1.0, 0.0)) for t in range(rows // LANES)],
        axis=1,
    )
    sorted_ref[...] = low(dot(order_mask, tokens_ref[...])).reshape(sorted_ref.shape)

    my_first = (x * extents[1] + y) * blocks
    for s, (inside, to_x, to_y) in enumerate(sides):
        bits = wanted_blocks(ids, counts, to_x, to_y, inside, my_first, blocks)
        ranks = ranks_of(bits)
        for r in range(CAP):
            pick = jnp.int32(0)
            for o in range(blocks):
                pick = jnp.where((bits[o] == 1) & (ranks[o] == r), o, pick)
            send[s, r] = sorted_ref[pick]
        for o in range(blocks):
            table_ref[blocks + o, s] = jnp.where(bits[o] == 1, s * CAP + ranks[o], 4 * CAP)

    copies = []
    for s, (inside, to_x, to_y) in enumerate(sides):
        copies.append(
            pltpu.make_async_remote_copy(
                src_ref=send.at[s],
                dst_ref=recv.at[s ^ 1],
                send_sem=send_sem.at[s],
                recv_sem=recv_sem.at[s ^ 1],
                device_id=(to_x, to_y),
                device_id_type=MESH,
            )
        )
    pl.semaphore_wait(barrier, peers_of(sides))

    for s, (inside, _, _) in enumerate(sides):

        @pl.when(inside)
        def _():
            copies[s].start()

        @pl.when(jnp.logical_not(inside))
        def _():
            recv[s] = jnp.zeros(recv.shape[1:], recv.dtype)

    bits = []
    firsts = []
    for inside, to_x, to_y in sides:
        firsts.append((to_x * extents[1] + to_y) * blocks)
        bits.append(wanted_blocks(ids, counts, x, y, inside, firsts[-1], blocks))
    ranks = [ranks_of(b) for b in bits]
    for b in range(blocks):
        table_ref[b, 0] = jnp.int32(b)
        table_ref[b, slots + 1] = counts[y, b, x]
        for j in range(slots):
            name = ids[y, b, j, x]
            at = name - my_first
            for s, (inside, _, _) in enumerate(sides):
                for o in range(blocks):
                    hit = inside & (name - firsts[s] == o)
                    at = jnp.where(hit, blocks + s * CAP + ranks[s][o], at)
            table_ref[b, j + 1] = at

    gain = gain_ref[...]
    pairs, lanes = q_ref.shape[0], q_ref.shape[2]

    def project(token_rows, place, count):
        values = token_rows.astype(jnp.float32)
        inv = lax.rsqrt(jnp.mean(values * values, axis=-1, keepdims=True) + EPSILON)
        normed = low(values * inv * gain)
        where = pl.ds(place, count)
        shape = (count, blk, features)
        normed_ref[where] = normed.reshape(shape)
        keys = low(dot(normed, w_qk_ref[:, features:]))
        values = low(dot(normed, w_value_ref[...]))
        for p in range(pairs):
            columns = slice(p * lanes, (p + 1) * lanes)
            kv_ref[p, where, :, :lanes] = keys[:, columns].reshape(count, blk, lanes)
            kv_ref[p, where, :, lanes:] = values[:, columns].reshape(count, blk, lanes)
        return normed

    normed = project(sorted_ref[...].reshape(rows, features), 0, blocks)
    query = low(dot(normed, w_qk_ref[:, :features]))
    cot = low(dot(order_mask, cotangent_ref[...]))
    cot_ref[...] = cot
    grad = low(dot_nt(cot, w_out_ref[...]))
    for p in range(pairs):
        q_ref[p] = query[:, p * lanes : (p + 1) * lanes]
        g_ref[p] = grad[:, p * lanes : (p + 1) * lanes]

    for s in (2, 3, 0, 1):

        @pl.when(sides[s][0])
        def _():
            copies[s ^ 1].wait_recv()

        project(recv[s].reshape(CAP * blk, features), blocks + s * CAP, CAP)
    for s in range(4):

        @pl.when(sides[s][0])
        def _():
            copies[s].wait_send()


def attend_kernel(
    table,
    q_ref,
    g_ref,
    kv_ref,
    normed_ref,
    cot_ref,
    w_qk_ref,
    w_value_ref,
    ctx_ref,
    dq_ref,
    shipped_ref,
    grad_ref,
    gain_ref,
    total,
    scores,
    slopes,
    lows,
    downs,
    turned_p,
    turned_d,
    *,
    factor,
):
    pairs, pool, blk, wide = kv_ref.shape
    rows, features = cot_ref.shape
    lanes = wide // 2
    half = lanes // 2
    blocks = rows // blk
    slots = lows.shape[0] // blk
    lane = lax.broadcasted_iota(jnp.int32, (1, lanes), 1)
    mine = [lane < half, lane >= half]

    def both(a):
        zero = jnp.zeros_like(a)
        return jnp.concatenate([jnp.where(m, a, zero) for m in mine], axis=0)

    def both_t(a):
        zero = jnp.zeros((half, blk), a.dtype)
        return jnp.concatenate(
            [
                jnp.concatenate([a[:half], zero], axis=0),
                jnp.concatenate([zero, a[half:]], axis=0),
            ],
            axis=1,
        )

    def body(pair, block, live):
        here = pl.ds(pl.multiple_of(block * blk, blk), blk)
        query = q_ref[pair, here, :] * jnp.asarray(factor, jnp.bfloat16)
        grad = g_ref[pair, here, :]
        q_cols, g_cols = both_t(query.T), both_t(grad.T)
        q_both, g_both = both(query), both(grad)
        at = [table[block, j] for j in range(live)]

        def part(j):
            return slice(j * blk, (j + 1) * blk)

        top = None
        for j in range(live):
            s_j = dot(kv_ref[pair, at[j], :, :lanes], q_cols)
            scores[part(j), :] = s_j
            m_j = jnp.max(s_j, axis=0, keepdims=True)
            top = m_j if j == 0 else jnp.maximum(top, m_j)
        for j in range(live):
            slope = dot(kv_ref[pair, at[j], :, lanes:], g_cols)
            slopes[part(j), :] = slope
            e_j = jnp.exp(scores[part(j), :] - top)
            scores[part(j), :] = e_j
            n_j = jnp.sum(e_j, axis=0, keepdims=True)
            c_j = jnp.sum(e_j * slope, axis=0, keepdims=True)
            norm = n_j if j == 0 else norm + n_j
            centre = c_j if j == 0 else centre + c_j
        inverse = 1.0 / norm
        centre = centre * inverse
        for j in range(live):
            p_j = scores[part(j), :] * inverse
            low_j = low(p_j)
            d_j = low(p_j * (slopes[part(j), :] - centre))
            lows[part(j), :] = low_j
            downs[part(j), :] = d_j
            for h in range(2):
                columns = slice((2 * j + h) * blk, (2 * j + h + 1) * blk)
                turned_p[:, columns] = low_j[:, h * blk : (h + 1) * blk].T
                turned_d[:, columns] = d_j[:, h * blk : (h + 1) * blk].T
            total[at[j], :, lanes:] += dot(lows[part(j), :], g_both)
            total[at[j], :, :lanes] += dot(downs[part(j), :], q_both)
        span = slice(0, 2 * live * blk)
        v_both = jnp.concatenate([both(kv_ref[pair, a, :, lanes:]) for a in at], axis=0)
        k_both = jnp.concatenate([both(kv_ref[pair, a, :, :lanes]) for a in at], axis=0)
        ctx_ref[pair, here, :] = low(dot(turned_p[:, span], v_both))
        dq_ref[pair, here, :] = low(dot(turned_d[:, span], k_both) * factor)

    normed = normed_ref[...].reshape(pool * blk, features)
    width = grad_ref.shape[1]
    span_rows = pairs * 4 * lanes

    def step(pair, _):
        for i in range(pool):
            total[i] = jnp.zeros(total.shape[1:], jnp.float32)

        def inner(block, _):
            count = table[block, slots]
            for live in range(2, slots + 1):
                pl.when(count == live - 1)(functools.partial(body, pair, block, live))
            return 0

        lax.fori_loop(0, blocks, inner, 0)
        shipped = low(total[...])
        shipped_ref[pair] = shipped
        parts = [
            dot_tn(dq_ref[pair], normed_ref[:blocks].reshape(rows, features)),
            dot_tn(shipped.reshape(pool * blk, wide), normed),
            dot_tn(ctx_ref[pair], cot_ref[...]),
        ]
        for c in range(features // width):
            start = 0
            for term in parts:
                size = term.shape[0]
                to = pl.multiple_of(c * span_rows + pair * 4 * lanes + start, lanes)
                grad_ref[pl.ds(to, size), :] = term[:, c * width : (c + 1) * width]
                start += size
        return 0

    lax.fori_loop(0, pairs, step, 0)
    for c in range(features // width):
        columns = slice(c * width, (c + 1) * width)
        gain = jnp.zeros((1, width), jnp.float32)
        for p in range(pairs):
            start = c * span_rows + p * 4 * lanes
            for part, (weight, first) in enumerate(
                ((w_qk_ref, 0), (w_qk_ref, features), (w_value_ref, 0))
            ):
                tile = grad_ref[start + part * lanes : start + (part + 1) * lanes, :]
                turned = weight[columns, first + p * lanes : first + (p + 1) * lanes].T
                gain += jnp.sum(tile * turned.astype(jnp.float32), axis=0, keepdims=True)
        gain_ref[:, columns] = jnp.broadcast_to(gain, (gain_ref.shape[0], width))


def exchange_kernel(
    table,
    grad_ref,
    shipped_ref,
    ctx_ref,
    dq_ref,
    w_qk_ref,
    w_value_ref,
    w_out_ref,
    sorted_ref,
    order_ref,
    gain_ref,
    gain_part,
    gathered,
    branch_ref,
    tokens_ref,
    gain_sum,
    gain_in,
    total,
    first_out,
    first_in,
    step_out,
    step_in,
    away,
    back,
    d_normed,
    d_rows,
    send_sem,
    recv_sem,
    gain_send,
    gain_recv,
    back_send,
    back_recv,
    *,
    extents,
):
    x, y = lax.axis_index("bx"), lax.axis_index("by")
    sides = sides_of(x, y, extents)
    blocks, blk, features = sorted_ref.shape
    rows = blocks * blk
    pairs = ctx_ref.shape[0]
    half = grad_ref.shape[0] // 2
    quarter = half // CHUNKS
    core = y % 2
    other_core = (x, y + 1 - 2 * core)
    groups = {
        "y": (extents[1] // 2, y // 2, lambda i: (x, 2 * i + core)),
        "near": (2, x % 2, lambda i: (x // 2 * 2 + i, y)),
        "far": (extents[0] // 2, x // 2, lambda i: (2 * i + x % 2, y)),
    }
    routes = [("y", "far", "near")] * CHUNKS
    sems = iter(range(send_sem.shape[0]))

    def remote(src, dst, to):
        sem = next(sems)
        return pltpu.make_async_remote_copy(
            src_ref=src,
            dst_ref=dst,
            send_sem=send_sem.at[sem],
            recv_sem=recv_sem.at[sem],
            device_id=to,
            device_id_type=MESH,
        )

    barrier = pltpu.get_barrier_semaphore()
    everyone = [other_core]
    for size, index, at in groups.values():
        everyone += [at((index + r) % size) for r in range(1, size)]
    for to in everyone:
        pl.semaphore_signal(barrier, inc=1, device_id=to, device_id_type=MESH)
    for inside, to_x, to_y in sides:

        @pl.when(inside)
        def _():
            pl.semaphore_signal(barrier, inc=1, device_id=(to_x, to_y), device_id_type=MESH)

    base = pl.multiple_of(core * half, half)
    give = pl.multiple_of((1 - core) * half, half)
    first_out[...] = low(grad_ref[pl.ds(give, half), :])
    pl.semaphore_wait(barrier, len(everyone) + peers_of(sides))

    started = []

    def launch(copy):
        copy.start()
        started.append(copy)
        return copy

    firsts = [
        launch(
            remote(
                first_out.at[pl.ds(way * quarter, quarter)],
                first_in.at[pl.ds(way * quarter, quarter)],
                other_core,
            )
        )
        for way in range(CHUNKS)
    ]

    weights = jnp.concatenate(
        [
            piece
            for p in range(pairs)
            for piece in (
                w_qk_ref[:, features + p * LANES : features + (p + 1) * LANES],
                w_value_ref[:, p * LANES : (p + 1) * LANES],
            )
        ],
        axis=1,
    )

    def kv_part(first, count):
        terms = [shipped_ref[p, first : first + count] for p in range(pairs)]
        joined = jnp.concatenate(terms, axis=-1).reshape(count * blk, pairs * 2 * LANES)
        return dot_nt(joined, weights)

    piece_rows = CAP * blk // PIECES
    per_block = PIECES // CAP
    returns = []
    for s, (inside, to_x, to_y) in enumerate(sides):
        returns.append(
            [
                pltpu.make_async_remote_copy(
                    src_ref=away.at[s, k // per_block, pl.ds(k % per_block * piece_rows, piece_rows)],
                    dst_ref=back.at[
                        (s ^ 1) * CAP + k // per_block,
                        pl.ds(k % per_block * piece_rows, piece_rows),
                    ],
                    send_sem=back_send.at[s, k],
                    recv_sem=back_recv.at[s ^ 1, k],
                    device_id=(to_x, to_y),
                    device_id_type=MESH,
                )
                for k in range(PIECES)
            ]
        )

    def make_away(s):
        away[s] = low(kv_part(blocks + s * CAP, CAP)).reshape(CAP, blk, features)

        @pl.when(jnp.logical_not(sides[s][0]))
        def _():
            back[pl.ds(s * CAP, CAP)] = jnp.zeros((CAP, blk, features), back.dtype)

    def send_back(s, first, count):
        @pl.when(sides[s][0])
        def _():
            for k in range(first, first + count):
                returns[s][k].start()

    offsets = [jnp.int32(way * quarter) for way in range(CHUNKS)]
    sizes = [quarter] * CHUNKS
    used = [0] * CHUNKS
    flying = [None] * CHUNKS

    def halve(way, name):
        count, index, at = groups[name]
        piece = sizes[way] // count
        off = pl.multiple_of(offsets[way], sizes[way])
        pos = used[way]
        step_out[way, pl.ds(pos, sizes[way]), :] = low(total[pl.ds(off, sizes[way]), :])
        flying[way] = [
            launch(
                remote(
                    step_out.at[
                        way,
                        pl.ds(pl.multiple_of(pos + (index + r) % count * piece, piece), piece),
                    ],
                    step_in.at[way, pl.ds(pos + r * piece, piece)],
                    at((index + r) % count),
                )
            )
            for r in range(1, count)
        ]

    def settle(way, name):
        count, index, _ = groups[name]
        piece = sizes[way] // count
        for copy in flying[way]:
            copy.wait_recv()
        offsets[way] = offsets[way] + index * piece
        here = pl.ds(pl.multiple_of(offsets[way], piece), piece)
        summed = total[here, :]
        for r in range(1, count):
            summed += step_in[way, pl.ds(used[way] + r * piece, piece), :].astype(jnp.float32)
        used[way] += sizes[way]
        sizes[way] = piece
        return here, summed

    def spread(way, name):
        count, index, at = groups[name]
        where = gathered.at[
            pl.ds(pl.multiple_of(base + offsets[way], sizes[way]), sizes[way])
        ]
        flying[way] = [
            launch(remote(where, where, at((index + r) % count))) for r in range(1, count)
        ]

    def spread_end(way, name):
        count, index, _ = groups[name]
        for copy in flying[way]:
            copy.wait_recv()
        offsets[way] = offsets[way] - index * sizes[way]
        sizes[way] *= count

    lasts = []

    def advance(way, step):
        route = routes[way]
        if step < 3:
            here, summed = settle(way, route[step])
            if step < 2:
                total[here, :] = summed
                halve(way, route[step + 1])
            else:
                to = pl.ds(pl.multiple_of(base + offsets[way], sizes[way]), sizes[way])
                gathered[to, :] = low(summed)
                spread(way, route[2])
        else:
            spread_end(way, route[5 - step])
            if step < 5:
                spread(way, route[4 - step])
            else:
                where = gathered.at[pl.ds(pl.multiple_of(base + way * quarter, quarter), quarter)]
                lasts.append(launch(remote(where, where, other_core)))

    def begin(way):
        halve(way, "y")

    def share(step, name):
        if name == "core":
            peers = [other_core]
        else:
            count, index, at = groups[name]
            peers = [at((index + r) % count) for r in range(1, count)]
        return [
            launch(
                pltpu.make_async_remote_copy(
                    src_ref=gain_sum.at[step],
                    dst_ref=gain_in.at[step, r],
                    send_sem=gain_send.at[step, r],
                    recv_sem=gain_recv.at[step, r],
                    device_id=to,
                    device_id_type=MESH,
                )
            )
            for r, to in enumerate(peers)
        ]

    def shared(step, copies):
        summed = gain_sum[step]
        for r, copy in enumerate(copies):
            copy.wait_recv()
            summed += gain_in[step, r]
        gain_sum[step + 1] = summed

    gain_sum[0] = gain_part[...]
    sharing = share(0, "core")
    make_away(0)
    make_away(1)
    for s in range(2):
        send_back(s, 0, FIRST_PIECES)
    for way in range(CHUNKS):
        firsts[way].wait_recv()
        span = pl.ds(way * quarter, quarter)
        mine = pl.ds(pl.multiple_of(base + way * quarter, quarter), quarter)
        total[span, :] = grad_ref[mine, :] + first_in[span, :].astype(jnp.float32)
        if way < 2:
            begin(way)
    make_away(2)
    make_away(3)
    for s in (2, 3):
        send_back(s, 0, PIECES)
    shared(0, sharing)
    sharing = share(1, "y")
    back[4 * CAP] = jnp.zeros((blk, features), back.dtype)

    order = order_ref[...]

    def unsort(rows_of, i):
        arrival = lax.broadcasted_iota(jnp.int32, (blk, rows), 0) + i * blk
        return dot(low(jnp.where(order == arrival, 1.0, 0.0)), rows_of)

    def own_part():
        d_normed[...] = kv_part(0, blocks)
        query_grad = jnp.concatenate([dq_ref[p] for p in range(pairs)], axis=1)
        d_normed[...] += dot_nt(query_grad, w_qk_ref[:, :features])

    def branch_part():
        context = jnp.concatenate([ctx_ref[p] for p in range(pairs)], axis=1)
        d_rows[:, :features] = low(dot(context, w_out_ref[...]))

    def branch_rows(i):
        branch_ref[i * blk : (i + 1) * blk, :] = low(unsort(d_rows[:, :features], i))

    tasks = [own_part, branch_part] + [
        functools.partial(branch_rows, i) for i in range(blocks)
    ]
    events = sorted(
        ((way, step) for way in range(CHUNKS) for step in range(6)),
        key=lambda e: (e[0] // 2 + e[1], e[0]),
    )
    first_late = next(n for n, e in enumerate(events) if e[0] // 2 + e[1] == 5)
    sent = FIRST_PIECES
    for way, step in events[:first_late]:
        advance(way, step)
        if step == 0 and way + 2 < CHUNKS:
            begin(way + 2)
        if sent < PIECES:
            for s in range(2):
                send_back(s, sent, PACE)
            sent += PACE
        if tasks:
            tasks.pop(0)()
    shared(1, sharing)
    sharing = share(2, "near")
    for task in tasks:
        task()

    for s in range(4):

        @pl.when(sides[s][0])
        def _():
            for k in range(PIECES):
                returns[s ^ 1][k].wait_recv()

    shared(2, sharing)
    sharing = share(3, "far")
    def token_rows(i):
        pieces = unsort(d_rows[...], i)
        tokens_ref[i * blk : (i + 1) * blk, :] = pieces[:, :features] + pieces[:, features:]

    gain = gain_ref[...]
    for o in range(blocks):
        here = slice(o * blk, (o + 1) * blk)
        slope = d_normed[here, :]
        for s in range(4):
            slope = slope + back[table[blocks + o, s]].astype(jnp.float32)
        values = sorted_ref[o].astype(jnp.float32)
        inv = lax.rsqrt(jnp.mean(values * values, axis=-1, keepdims=True) + EPSILON)
        scaled = slope * gain
        inner = jnp.mean(values * scaled, axis=-1, keepdims=True)
        result = inv * scaled - values * ((inv * inv * inv) * inner)
        top = low(result)
        d_rows[here, :features] = top
        d_rows[here, features:] = low(result - top.astype(jnp.float32))

    for n, (way, step) in enumerate(events[first_late:]):
        advance(way, step)
        if n < blocks:
            token_rows(n)
    for n in range(len(events) - first_late, blocks):
        token_rows(n)
    shared(3, sharing)
    for copy in lasts:
        copy.wait_recv()
    for copy in started:
        copy.wait_send()
    for s in range(4):

        @pl.when(sides[s][0])
        def _():
            for k in range(PIECES):
                returns[s][k].wait_send()


def finish_kernel(
    gathered, gain_sum, gain_ref, grad_qk_ref, grad_value_ref, grad_out_ref, grad_gain_ref
):
    features = grad_out_ref.shape[0]
    width = gathered.shape[1]
    pairs = HEADS // 2
    lanes = features // pairs
    for c in range(features // width):
        wide = slice(c * width, (c + 1) * width)
        for p in range(pairs):
            start = (c * pairs + p) * 4 * lanes
            for part, (first, out) in enumerate(
                ((0, grad_qk_ref), (features, grad_qk_ref), (0, grad_value_ref))
            ):
                tile = gathered[start + part * lanes : start + (part + 1) * lanes, :]
                out[wide, first + p * lanes : first + (p + 1) * lanes] = tile.T.astype(
                    jnp.float32
                )
            grad_out_ref[p * lanes : (p + 1) * lanes, wide] = gathered[
                start + 3 * lanes : start + 4 * lanes, :
            ].astype(jnp.float32)
    last = gain_sum.shape[0] - 1
    grad_gain_ref[...] = gain_sum[last, 0:1] / gain_ref[...]


F32, BF16 = jnp.float32, jnp.bfloat16
ON_CHIP = pl.BlockSpec(memory_space=pltpu.VMEM)
SCALARS = pl.BlockSpec(memory_space=pltpu.SMEM)


def attend_call(table, query, d_context, key_value, normed, cot, w_query_key, w_value):
    pairs, pool, _, wide = key_value.shape
    rows, features = cot.shape
    slots = table.shape[1] - 1
    return pl.pallas_call(
        functools.partial(attend_kernel, factor=1.0 / math.sqrt(features // HEADS)),
        out_shape=[
            pltpu.VMEM((pairs, rows, wide // 2), BF16),
            pltpu.VMEM((pairs, rows, wide // 2), BF16),
            pltpu.VMEM((pairs, pool, BLK, wide), BF16),
            pltpu.VMEM((4 * features * (features // LANES), LANES), F32),
            pltpu.VMEM((8, features), F32),
        ],
        in_specs=[SCALARS] + [ON_CHIP] * 7,
        out_specs=[ON_CHIP] * 5,
        scratch_shapes=[
            pltpu.VMEM((pool, BLK, wide), F32),
            pltpu.VMEM((slots * BLK, 2 * BLK), F32),
            pltpu.VMEM((slots * BLK, 2 * BLK), F32),
            pltpu.VMEM((slots * BLK, 2 * BLK), BF16),
            pltpu.VMEM((slots * BLK, 2 * BLK), BF16),
            pltpu.VMEM((BLK, slots * 2 * BLK), BF16),
            pltpu.VMEM((BLK, slots * 2 * BLK), BF16),
        ],
        compiler_params=pltpu.CompilerParams(vmem_limit_bytes=24 << 20),
        name="attend",
    )(table, query, d_context, key_value, normed, cot, w_query_key, w_value)


def shards(
    tokens,
    norm_gain,
    w_query_key,
    w_value,
    w_out,
    cotangent,
    block_order,
    neighbour_ids,
    neighbour_count,
):
    rows, features = tokens.shape[2:]
    blocks = rows // BLK
    slots = neighbour_ids.shape[3] + 1
    extents = (lax.axis_size("bx"), lax.axis_size("by"))
    pairs = HEADS // 2
    lanes = features // pairs
    pool = blocks + 4 * CAP
    gain = norm_gain.reshape(1, features)
    order = block_order.reshape(1, rows)
    dma = pltpu.SemaphoreType.DMA

    table, sorted_rows, cot, normed, query, d_context, key_value = pl.pallas_call(
        functools.partial(fetch_kernel, extents=extents),
        out_shape=[
            jax.ShapeDtypeStruct((2 * blocks, slots + 1), jnp.int32),
            pltpu.VMEM((blocks, BLK, features), BF16),
            pltpu.VMEM((rows, features), BF16),
            pltpu.VMEM((pool, BLK, features), BF16),
            pltpu.VMEM((pairs, rows, lanes), BF16),
            pltpu.VMEM((pairs, rows, lanes), BF16),
            pltpu.VMEM((pairs, pool, BLK, 2 * lanes), BF16),
        ],
        in_specs=[SCALARS] * 2 + [ON_CHIP] * 7,
        out_specs=[SCALARS] + [ON_CHIP] * 6,
        scratch_shapes=[
            pltpu.VMEM((4, CAP, BLK, features), BF16),
            pltpu.VMEM((4, CAP, BLK, features), BF16),
            dma((4,)),
            dma((4,)),
        ],
        compiler_params=pltpu.CompilerParams(
            collective_id=0, has_side_effects=True, vmem_limit_bytes=30 << 20
        ),
        name="fetch",
    )(
        neighbour_ids.transpose(1, 2, 3, 0),
        neighbour_count.transpose(1, 2, 0),
        order,
        tokens[0, 0],
        cotangent[0, 0],
        gain,
        w_query_key,
        w_value,
        w_out,
    )
    context, d_query, shipped, grads, gain_part = attend_call(
        table, query, d_context, key_value, normed, cot, w_query_key, w_value
    )

    grad_rows = 4 * features * (features // LANES)
    half = grad_rows // 2
    most = max(extents[0] // 2, extents[1] // 2, 2) - 1
    messages = CHUNKS * (2 + 2 * (extents[0] // 2 + extents[1] // 2 - 1))
    gathered, branch, grad_tokens, gain_sum = pl.pallas_call(
        functools.partial(exchange_kernel, extents=extents),
        out_shape=[
            pltpu.VMEM((grad_rows, LANES), BF16),
            pltpu.VMEM((rows, features), BF16),
            pltpu.VMEM((rows, features), F32),
            pltpu.VMEM((5, 8, features), F32),
        ],
        in_specs=[SCALARS] + [ON_CHIP] * 11,
        out_specs=[ON_CHIP] * 4,
        scratch_shapes=[
            pltpu.VMEM((4, most, 8, features), F32),
            pltpu.VMEM((half, LANES), F32),
            pltpu.VMEM((half, LANES), BF16),
            pltpu.VMEM((half, LANES), BF16),
            pltpu.VMEM((CHUNKS, 2 * half // CHUNKS, LANES), BF16),
            pltpu.VMEM((CHUNKS, 2 * half // CHUNKS, LANES), BF16),
            pltpu.VMEM((4, CAP, BLK, features), BF16),
            pltpu.VMEM((4 * CAP + 1, BLK, features), BF16),
            pltpu.VMEM((rows, features), F32),
            pltpu.VMEM((rows, 2 * features), BF16),
            dma((messages,)),
            dma((messages,)),
            dma((4, most)),
            dma((4, most)),
            dma((4, PIECES)),
            dma((4, PIECES)),
        ],
        compiler_params=pltpu.CompilerParams(
            collective_id=1, has_side_effects=True, vmem_limit_bytes=30 << 20
        ),
        name="exchange",
    )(
        table,
        grads,
        shipped,
        context,
        d_query,
        w_query_key,
        w_value,
        w_out,
        sorted_rows,
        order,
        gain,
        gain_part,
    )

    shape = jax.ShapeDtypeStruct
    grad_qk, grad_value, grad_out, grad_gain = pl.pallas_call(
        finish_kernel,
        out_shape=[
            shape((features, 2 * features), F32),
            shape((features, features), F32),
            shape((features, features), F32),
            shape((1, features), F32),
        ],
        in_specs=[ON_CHIP] * 3,
        out_specs=[ON_CHIP] * 4,
        compiler_params=pltpu.CompilerParams(vmem_limit_bytes=24 << 20),
        name="finish",
    )(gathered, gain_sum, gain)
    return (
        branch[None, None],
        grad_tokens[None, None],
        grad_qk,
        grad_value,
        grad_out,
        grad_gain.reshape(features),
    )


def solution(mesh):
    bricks = P("bx", "by", None, None)
    placed = (bricks, P(), P(), P(), P(), bricks, P("bx", "by", None), P(), P())
    return jax.shard_map(
        shards,
        mesh=mesh,
        in_specs=placed,
        out_specs=(bricks, bricks, P(), P(), P(), P()),
        check_vma=False,
    )
```

```python
import functools
import math

import jax
import jax.numpy as jnp
from jax import lax
from jax.experimental import pallas as pl
from jax.experimental.pallas import tpu as pltpu
from jax.sharding import PartitionSpec as P

HEADS = 8
BLK = 256
CAP = 2
LANES = 128
CHUNKS = 4
PIECES = 8
FIRST_PIECES = 1
PACE = 1
EPSILON = 1e-06
MESH = pl.DeviceIdType.MESH
SIDES = ((-1, 0), (1, 0), (0, -1), (0, 1))


def dot(a, b):
    return jnp.dot(a, b, preferred_element_type=jnp.float32)


def dot_nt(a, b):
    return lax.dot_general(a, b, (((1,), (1,)), ((), ())), preferred_element_type=jnp.float32)


def dot_tn(a, b):
    return lax.dot_general(a, b, (((0,), (0,)), ((), ())), preferred_element_type=jnp.float32)


def low(a):
    return a.astype(jnp.bfloat16)


def sides_of(x, y, extents):
    found = []
    for step_x, step_y in SIDES:
        to_x, to_y = x + step_x, y + step_y
        inside = (to_x >= 0) & (to_x < extents[0]) & (to_y >= 0) & (to_y < extents[1])
        found.append(
            (inside, jnp.clip(to_x, 0, extents[0] - 1), jnp.clip(to_y, 0, extents[1] - 1))
        )
    return found


def peers_of(sides):
    return sum(jnp.where(inside, 1, 0) for inside, _, _ in sides)


def wanted_blocks(ids, counts, x, y, inside, first_id, blocks):
    bits = [jnp.int32(0)] * blocks
    for b in range(blocks):
        live = counts[y, b, x]
        for j in range(ids.shape[2]):
            offset = ids[y, b, j, x] - first_id
            hit = inside & (j < live)
            bits = [jnp.where(hit & (offset == o), 1, bits[o]) for o in range(blocks)]
    return bits


def ranks_of(bits):
    ranks, count = [], jnp.int32(0)
    for bit in bits:
        ranks.append(count)
        count = count + bit
    return ranks


def fetch_kernel(
    ids_in,
    counts_in,
    order_in,
    tokens_in,
    cotangent_in,
    gain_in,
    w_qk_in,
    w_value_in,
    w_out_in,
    table_ref,
    sorted_ref,
    cot_ref,
    normed_ref,
    q_ref,
    g_ref,
    kv_ref,
    ids,
    counts,
    order_ref,
    tokens_ref,
    cotangent_ref,
    gain_ref,
    w_qk_ref,
    w_value_ref,
    w_out_ref,
    send,
    recv,
    load_sem,
    send_sem,
    recv_sem,
    *,
    extents,
):
    pairs_of = (
        (order_in, order_ref),
        (tokens_in, tokens_ref),
        (ids_in, ids),
        (counts_in, counts),
        (gain_in, gain_ref),
        (w_qk_in, w_qk_ref),
        (w_value_in, w_value_ref),
        (cotangent_in, cotangent_ref),
        (w_out_in, w_out_ref),
    )
    loads = [
        pltpu.make_async_copy(src, dst, load_sem.at[n]) for n, (src, dst) in enumerate(pairs_of)
    ]
    for load in loads:
        load.start()
    x, y = lax.axis_index("bx"), lax.axis_index("by")
    sides = sides_of(x, y, extents)
    blocks, blk, features = sorted_ref.shape
    rows = blocks * blk
    slots = ids.shape[2]

    barrier = pltpu.get_barrier_semaphore()
    for inside, to_x, to_y in sides:

        @pl.when(inside)
        def _():
            pl.semaphore_signal(barrier, inc=1, device_id=(to_x, to_y), device_id_type=MESH)

    loads[0].wait()
    order = jnp.broadcast_to(order_ref[...].astype(jnp.float32), (LANES, rows)).T
    lane = lax.broadcasted_iota(jnp.int32, (rows, LANES), 1).astype(jnp.float32)
    order_mask = jnp.concatenate(
        [low(jnp.where(order == lane + t * LANES, 1.0, 0.0)) for t in range(rows // LANES)],
        axis=1,
    )
    for load in loads[1:4]:
        load.wait()
    sorted_ref[...] = low(dot(order_mask, tokens_ref[...])).reshape(sorted_ref.shape)

    my_first = (x * extents[1] + y) * blocks
    for s, (inside, to_x, to_y) in enumerate(sides):
        bits = wanted_blocks(ids, counts, to_x, to_y, inside, my_first, blocks)
        ranks = ranks_of(bits)
        for r in range(CAP):
            pick = jnp.int32(0)
            for o in range(blocks):
                pick = jnp.where((bits[o] == 1) & (ranks[o] == r), o, pick)
            send[s, r] = sorted_ref[pick]
        for o in range(blocks):
            table_ref[blocks + o, s] = jnp.where(bits[o] == 1, s * CAP + ranks[o], 4 * CAP)

    copies = []
    for s, (inside, to_x, to_y) in enumerate(sides):
        copies.append(
            pltpu.make_async_remote_copy(
                src_ref=send.at[s],
                dst_ref=recv.at[s ^ 1],
                send_sem=send_sem.at[s],
                recv_sem=recv_sem.at[s ^ 1],
                device_id=(to_x, to_y),
                device_id_type=MESH,
            )
        )
    pl.semaphore_wait(barrier, peers_of(sides))

    for s, (inside, _, _) in enumerate(sides):

        @pl.when(inside)
        def _():
            copies[s].start()

        @pl.when(jnp.logical_not(inside))
        def _():
            recv[s] = jnp.zeros(recv.shape[1:], recv.dtype)

    bits = []
    firsts = []
    for inside, to_x, to_y in sides:
        firsts.append((to_x * extents[1] + to_y) * blocks)
        bits.append(wanted_blocks(ids, counts, x, y, inside, firsts[-1], blocks))
    ranks = [ranks_of(b) for b in bits]
    for b in range(blocks):
        table_ref[b, 0] = jnp.int32(b)
        table_ref[b, slots + 1] = counts[y, b, x]
        for j in range(slots):
            name = ids[y, b, j, x]
            at = name - my_first
            for s, (inside, _, _) in enumerate(sides):
                for o in range(blocks):
                    hit = inside & (name - firsts[s] == o)
                    at = jnp.where(hit, blocks + s * CAP + ranks[s][o], at)
            table_ref[b, j + 1] = at

    for load in loads[4:]:
        load.wait()
    gain = gain_ref[...]
    pairs, lanes = q_ref.shape[0], q_ref.shape[2]

    def project(token_rows, place, count):
        values = token_rows.astype(jnp.float32)
        inv = lax.rsqrt(jnp.mean(values * values, axis=-1, keepdims=True) + EPSILON)
        normed = low(values * inv * gain)
        where = pl.ds(place, count)
        shape = (count, blk, features)
        normed_ref[where] = normed.reshape(shape)
        keys = low(dot(normed, w_qk_ref[:, features:]))
        values = low(dot(normed, w_value_ref[...]))
        for p in range(pairs):
            columns = slice(p * lanes, (p + 1) * lanes)
            kv_ref[p, where, :, :lanes] = keys[:, columns].reshape(count, blk, lanes)
            kv_ref[p, where, :, lanes:] = values[:, columns].reshape(count, blk, lanes)
        return normed

    normed = project(sorted_ref[...].reshape(rows, features), 0, blocks)
    query = low(dot(normed, w_qk_ref[:, :features]))
    cot = low(dot(order_mask, cotangent_ref[...]))
    cot_ref[...] = cot
    grad = low(dot_nt(cot, w_out_ref[...]))
    for p in range(pairs):
        q_ref[p] = query[:, p * lanes : (p + 1) * lanes]
        g_ref[p] = grad[:, p * lanes : (p + 1) * lanes]

    for s in (2, 3, 0, 1):

        @pl.when(sides[s][0])
        def _():
            copies[s ^ 1].wait_recv()

        project(recv[s].reshape(CAP * blk, features), blocks + s * CAP, CAP)
    for s in range(4):

        @pl.when(sides[s][0])
        def _():
            copies[s].wait_send()


def attend_kernel(
    table,
    q_ref,
    g_ref,
    kv_ref,
    normed_ref,
    cot_ref,
    w_qk_ref,
    w_value_ref,
    ctx_ref,
    dq_ref,
    shipped_ref,
    grad_ref,
    gain_ref,
    total,
    scores,
    slopes,
    lows,
    downs,
    turned_p,
    turned_d,
    *,
    factor,
):
    pairs, pool, blk, wide = kv_ref.shape
    rows, features = cot_ref.shape
    lanes = wide // 2
    half = lanes // 2
    blocks = rows // blk
    slots = lows.shape[0] // blk
    lane = lax.broadcasted_iota(jnp.int32, (1, lanes), 1)
    mine = [lane < half, lane >= half]

    def both(a):
        zero = jnp.zeros_like(a)
        return jnp.concatenate([jnp.where(m, a, zero) for m in mine], axis=0)

    def both_t(a):
        zero = jnp.zeros((half, blk), a.dtype)
        return jnp.concatenate(
            [
                jnp.concatenate([a[:half], zero], axis=0),
                jnp.concatenate([zero, a[half:]], axis=0),
            ],
            axis=1,
        )

    def body(pair, block, live):
        here = pl.ds(pl.multiple_of(block * blk, blk), blk)
        query = q_ref[pair, here, :] * jnp.asarray(factor, jnp.bfloat16)
        grad = g_ref[pair, here, :]
        q_cols, g_cols = both_t(query.T), both_t(grad.T)
        q_both, g_both = both(query), both(grad)
        at = [table[block, j] for j in range(live)]

        def part(j):
            return slice(j * blk, (j + 1) * blk)

        top = None
        for j in range(live):
            s_j = dot(kv_ref[pair, at[j], :, :lanes], q_cols)
            scores[part(j), :] = s_j
            m_j = jnp.max(s_j, axis=0, keepdims=True)
            top = m_j if j == 0 else jnp.maximum(top, m_j)
        for j in range(live):
            slope = dot(kv_ref[pair, at[j], :, lanes:], g_cols)
            slopes[part(j), :] = slope
            e_j = jnp.exp(scores[part(j), :] - top)
            scores[part(j), :] = e_j
            n_j = jnp.sum(e_j, axis=0, keepdims=True)
            c_j = jnp.sum(e_j * slope, axis=0, keepdims=True)
            norm = n_j if j == 0 else norm + n_j
            centre = c_j if j == 0 else centre + c_j
        inverse = 1.0 / norm
        centre = centre * inverse
        for j in range(live):
            p_j = scores[part(j), :] * inverse
            low_j = low(p_j)
            d_j = low(p_j * (slopes[part(j), :] - centre))
            lows[part(j), :] = low_j
            downs[part(j), :] = d_j
            for h in range(2):
                columns = slice((2 * j + h) * blk, (2 * j + h + 1) * blk)
                turned_p[:, columns] = low_j[:, h * blk : (h + 1) * blk].T
                turned_d[:, columns] = d_j[:, h * blk : (h + 1) * blk].T
            total[at[j], :, lanes:] += dot(lows[part(j), :], g_both)
            total[at[j], :, :lanes] += dot(downs[part(j), :], q_both)
        span = slice(0, 2 * live * blk)
        v_both = jnp.concatenate([both(kv_ref[pair, a, :, lanes:]) for a in at], axis=0)
        k_both = jnp.concatenate([both(kv_ref[pair, a, :, :lanes]) for a in at], axis=0)
        ctx_ref[pair, here, :] = low(dot(turned_p[:, span], v_both))
        dq_ref[pair, here, :] = low(dot(turned_d[:, span], k_both) * factor)

    normed = normed_ref[...].reshape(pool * blk, features)
    width = grad_ref.shape[1]
    span_rows = pairs * 4 * lanes

    def step(pair, _):
        for i in range(pool):
            total[i] = jnp.zeros(total.shape[1:], jnp.float32)

        def inner(block, _):
            count = table[block, slots]
            for live in range(2, slots + 1):
                pl.when(count == live - 1)(functools.partial(body, pair, block, live))
            return 0

        lax.fori_loop(0, blocks, inner, 0)
        shipped = low(total[...])
        shipped_ref[pair] = shipped
        parts = [
            dot_tn(dq_ref[pair], normed_ref[:blocks].reshape(rows, features)),
            dot_tn(shipped.reshape(pool * blk, wide), normed),
            dot_tn(ctx_ref[pair], cot_ref[...]),
        ]
        for c in range(features // width):
            start = 0
            for term in parts:
                size = term.shape[0]
                to = pl.multiple_of(c * span_rows + pair * 4 * lanes + start, lanes)
                grad_ref[pl.ds(to, size), :] = term[:, c * width : (c + 1) * width]
                start += size
        return 0

    lax.fori_loop(0, pairs, step, 0)
    for c in range(features // width):
        columns = slice(c * width, (c + 1) * width)
        gain = jnp.zeros((1, width), jnp.float32)
        for p in range(pairs):
            start = c * span_rows + p * 4 * lanes
            for part, (weight, first) in enumerate(
                ((w_qk_ref, 0), (w_qk_ref, features), (w_value_ref, 0))
            ):
                tile = grad_ref[start + part * lanes : start + (part + 1) * lanes, :]
                turned = weight[columns, first + p * lanes : first + (p + 1) * lanes].T
                gain += jnp.sum(tile * turned.astype(jnp.float32), axis=0, keepdims=True)
        gain_ref[:, columns] = jnp.broadcast_to(gain, (gain_ref.shape[0], width))


def exchange_kernel(
    table,
    grad_ref,
    shipped_ref,
    ctx_ref,
    dq_ref,
    w_qk_ref,
    w_value_ref,
    w_out_ref,
    sorted_ref,
    order_ref,
    gain_ref,
    gain_part,
    gathered,
    branch_ref,
    tokens_ref,
    gain_sum,
    gain_in,
    total,
    first_out,
    first_in,
    step_out,
    step_in,
    away,
    back,
    d_normed,
    d_rows,
    send_sem,
    recv_sem,
    gain_send,
    gain_recv,
    back_send,
    back_recv,
    *,
    extents,
):
    x, y = lax.axis_index("bx"), lax.axis_index("by")
    sides = sides_of(x, y, extents)
    blocks, blk, features = sorted_ref.shape
    rows = blocks * blk
    pairs = ctx_ref.shape[0]
    half = grad_ref.shape[0] // 2
    quarter = half // CHUNKS
    core = y % 2
    other_core = (x, y + 1 - 2 * core)
    groups = {
        "y": (extents[1] // 2, y // 2, lambda i: (x, 2 * i + core)),
        "near": (2, x % 2, lambda i: (x // 2 * 2 + i, y)),
        "far": (extents[0] // 2, x // 2, lambda i: (2 * i + x % 2, y)),
    }
    routes = [("y", "far", "near")] * CHUNKS
    sems = iter(range(send_sem.shape[0]))

    def remote(src, dst, to):
        sem = next(sems)
        return pltpu.make_async_remote_copy(
            src_ref=src,
            dst_ref=dst,
            send_sem=send_sem.at[sem],
            recv_sem=recv_sem.at[sem],
            device_id=to,
            device_id_type=MESH,
        )

    barrier = pltpu.get_barrier_semaphore()
    everyone = [other_core]
    for size, index, at in groups.values():
        everyone += [at((index + r) % size) for r in range(1, size)]
    for to in everyone:
        pl.semaphore_signal(barrier, inc=1, device_id=to, device_id_type=MESH)
    for inside, to_x, to_y in sides:

        @pl.when(inside)
        def _():
            pl.semaphore_signal(barrier, inc=1, device_id=(to_x, to_y), device_id_type=MESH)

    base = pl.multiple_of(core * half, half)
    give = pl.multiple_of((1 - core) * half, half)
    first_out[...] = low(grad_ref[pl.ds(give, half), :])
    pl.semaphore_wait(barrier, len(everyone) + peers_of(sides))

    started = []

    def launch(copy):
        copy.start()
        started.append(copy)
        return copy

    firsts = [
        launch(
            remote(
                first_out.at[pl.ds(way * quarter, quarter)],
                first_in.at[pl.ds(way * quarter, quarter)],
                other_core,
            )
        )
        for way in range(CHUNKS)
    ]

    weights = jnp.concatenate(
        [
            piece
            for p in range(pairs)
            for piece in (
                w_qk_ref[:, features + p * LANES : features + (p + 1) * LANES],
                w_value_ref[:, p * LANES : (p + 1) * LANES],
            )
        ],
        axis=1,
    )

    def kv_part(first, count):
        terms = [shipped_ref[p, first : first + count] for p in range(pairs)]
        joined = jnp.concatenate(terms, axis=-1).reshape(count * blk, pairs * 2 * LANES)
        return dot_nt(joined, weights)

    piece_rows = CAP * blk // PIECES
    per_block = PIECES // CAP
    returns = []
    for s, (inside, to_x, to_y) in enumerate(sides):
        returns.append(
            [
                pltpu.make_async_remote_copy(
                    src_ref=away.at[s, k // per_block, pl.ds(k % per_block * piece_rows, piece_rows)],
                    dst_ref=back.at[
                        (s ^ 1) * CAP + k // per_block,
                        pl.ds(k % per_block * piece_rows, piece_rows),
                    ],
                    send_sem=back_send.at[s, k],
                    recv_sem=back_recv.at[s ^ 1, k],
                    device_id=(to_x, to_y),
                    device_id_type=MESH,
                )
                for k in range(PIECES)
            ]
        )

    def make_away(s):
        away[s] = low(kv_part(blocks + s * CAP, CAP)).reshape(CAP, blk, features)

        @pl.when(jnp.logical_not(sides[s][0]))
        def _():
            back[pl.ds(s * CAP, CAP)] = jnp.zeros((CAP, blk, features), back.dtype)

    def send_back(s, first, count):
        @pl.when(sides[s][0])
        def _():
            for k in range(first, first + count):
                returns[s][k].start()

    offsets = [jnp.int32(way * quarter) for way in range(CHUNKS)]
    sizes = [quarter] * CHUNKS
    used = [0] * CHUNKS
    flying = [None] * CHUNKS

    def halve(way, name):
        count, index, at = groups[name]
        piece = sizes[way] // count
        off = pl.multiple_of(offsets[way], sizes[way])
        pos = used[way]
        step_out[way, pl.ds(pos, sizes[way]), :] = low(total[pl.ds(off, sizes[way]), :])
        flying[way] = [
            launch(
                remote(
                    step_out.at[
                        way,
                        pl.ds(pl.multiple_of(pos + (index + r) % count * piece, piece), piece),
                    ],
                    step_in.at[way, pl.ds(pos + r * piece, piece)],
                    at((index + r) % count),
                )
            )
            for r in range(1, count)
        ]

    def settle(way, name):
        count, index, _ = groups[name]
        piece = sizes[way] // count
        for copy in flying[way]:
            copy.wait_recv()
        offsets[way] = offsets[way] + index * piece
        here = pl.ds(pl.multiple_of(offsets[way], piece), piece)
        summed = total[here, :]
        for r in range(1, count):
            summed += step_in[way, pl.ds(used[way] + r * piece, piece), :].astype(jnp.float32)
        used[way] += sizes[way]
        sizes[way] = piece
        return here, summed

    def spread(way, name):
        count, index, at = groups[name]
        where = gathered.at[
            pl.ds(pl.multiple_of(base + offsets[way], sizes[way]), sizes[way])
        ]
        flying[way] = [
            launch(remote(where, where, at((index + r) % count))) for r in range(1, count)
        ]

    def spread_end(way, name):
        count, index, _ = groups[name]
        for copy in flying[way]:
            copy.wait_recv()
        offsets[way] = offsets[way] - index * sizes[way]
        sizes[way] *= count

    lasts = []

    def advance(way, step):
        route = routes[way]
        if step < 3:
            here, summed = settle(way, route[step])
            if step < 2:
                total[here, :] = summed
                halve(way, route[step + 1])
            else:
                to = pl.ds(pl.multiple_of(base + offsets[way], sizes[way]), sizes[way])
                gathered[to, :] = low(summed)
                spread(way, route[2])
        else:
            spread_end(way, route[5 - step])
            if step < 5:
                spread(way, route[4 - step])
            else:
                where = gathered.at[pl.ds(pl.multiple_of(base + way * quarter, quarter), quarter)]
                lasts.append(launch(remote(where, where, other_core)))

    def begin(way):
        halve(way, "y")

    def share(step, name):
        if name == "core":
            peers = [other_core]
        else:
            count, index, at = groups[name]
            peers = [at((index + r) % count) for r in range(1, count)]
        return [
            launch(
                pltpu.make_async_remote_copy(
                    src_ref=gain_sum.at[step],
                    dst_ref=gain_in.at[step, r],
                    send_sem=gain_send.at[step, r],
                    recv_sem=gain_recv.at[step, r],
                    device_id=to,
                    device_id_type=MESH,
                )
            )
            for r, to in enumerate(peers)
        ]

    def shared(step, copies):
        summed = gain_sum[step]
        for r, copy in enumerate(copies):
            copy.wait_recv()
            summed += gain_in[step, r]
        gain_sum[step + 1] = summed

    gain_sum[0] = gain_part[...]
    sharing = share(0, "core")
    make_away(0)
    make_away(1)
    for s in range(2):
        send_back(s, 0, FIRST_PIECES)
    for way in range(CHUNKS):
        firsts[way].wait_recv()
        span = pl.ds(way * quarter, quarter)
        mine = pl.ds(pl.multiple_of(base + way * quarter, quarter), quarter)
        total[span, :] = grad_ref[mine, :] + first_in[span, :].astype(jnp.float32)
        if way < 2:
            begin(way)
    make_away(2)
    make_away(3)
    for s in (2, 3):
        send_back(s, 0, PIECES)
    shared(0, sharing)
    sharing = share(1, "y")
    back[4 * CAP] = jnp.zeros((blk, features), back.dtype)

    order = order_ref[...]

    def unsort(rows_of, i):
        arrival = lax.broadcasted_iota(jnp.int32, (blk, rows), 0) + i * blk
        return dot(low(jnp.where(order == arrival, 1.0, 0.0)), rows_of)

    def own_part():
        d_normed[...] = kv_part(0, blocks)
        query_grad = jnp.concatenate([dq_ref[p] for p in range(pairs)], axis=1)
        d_normed[...] += dot_nt(query_grad, w_qk_ref[:, :features])

    def branch_part():
        context = jnp.concatenate([ctx_ref[p] for p in range(pairs)], axis=1)
        d_rows[:, :features] = low(dot(context, w_out_ref[...]))

    def branch_rows(i):
        branch_ref[i * blk : (i + 1) * blk, :] = low(unsort(d_rows[:, :features], i))

    tasks = [own_part, branch_part] + [
        functools.partial(branch_rows, i) for i in range(blocks)
    ]
    events = sorted(
        ((way, step) for way in range(CHUNKS) for step in range(6)),
        key=lambda e: (e[0] // 2 + e[1], e[0]),
    )
    first_late = next(n for n, e in enumerate(events) if e[0] // 2 + e[1] == 5)
    sent = FIRST_PIECES
    for way, step in events[:first_late]:
        advance(way, step)
        if step == 0 and way + 2 < CHUNKS:
            begin(way + 2)
        if sent < PIECES:
            for s in range(2):
                send_back(s, sent, PACE)
            sent += PACE
        if tasks:
            tasks.pop(0)()
    shared(1, sharing)
    sharing = share(2, "near")
    for task in tasks:
        task()

    for s in range(4):

        @pl.when(sides[s][0])
        def _():
            for k in range(PIECES):
                returns[s ^ 1][k].wait_recv()

    shared(2, sharing)
    sharing = share(3, "far")
    def token_rows(i):
        pieces = unsort(d_rows[...], i)
        tokens_ref[i * blk : (i + 1) * blk, :] = pieces[:, :features] + pieces[:, features:]

    gain = gain_ref[...]
    for o in range(blocks):
        here = slice(o * blk, (o + 1) * blk)
        slope = d_normed[here, :]
        for s in range(4):
            slope = slope + back[table[blocks + o, s]].astype(jnp.float32)
        values = sorted_ref[o].astype(jnp.float32)
        inv = lax.rsqrt(jnp.mean(values * values, axis=-1, keepdims=True) + EPSILON)
        scaled = slope * gain
        inner = jnp.mean(values * scaled, axis=-1, keepdims=True)
        result = inv * scaled - values * ((inv * inv * inv) * inner)
        top = low(result)
        d_rows[here, :features] = top
        d_rows[here, features:] = low(result - top.astype(jnp.float32))

    for n, (way, step) in enumerate(events[first_late:]):
        advance(way, step)
        if n < blocks:
            token_rows(n)
    for n in range(len(events) - first_late, blocks):
        token_rows(n)
    shared(3, sharing)
    for copy in lasts:
        copy.wait_recv()
    for copy in started:
        copy.wait_send()
    for s in range(4):

        @pl.when(sides[s][0])
        def _():
            for k in range(PIECES):
                returns[s][k].wait_send()


def finish_kernel(
    gathered,
    gain_sum,
    gain_ref,
    branch_ref,
    tokens_ref,
    grad_qk_out,
    grad_value_out,
    grad_out_out,
    grad_gain_ref,
    branch_out,
    tokens_out,
    grad_qk_ref,
    grad_value_ref,
    grad_out_ref,
    sem,
):
    moves = [
        pltpu.make_async_copy(src, dst, sem.at[n])
        for n, (src, dst) in enumerate(
            (
                (tokens_ref, tokens_out),
                (branch_ref, branch_out),
                (grad_qk_ref, grad_qk_out),
                (grad_value_ref, grad_value_out),
                (grad_out_ref, grad_out_out),
            )
        )
    ]
    moves[0].start()
    moves[1].start()
    features = grad_out_ref.shape[0]
    width = gathered.shape[1]
    pairs = HEADS // 2
    lanes = features // pairs
    for c in range(features // width):
        wide = slice(c * width, (c + 1) * width)
        for p in range(pairs):
            start = (c * pairs + p) * 4 * lanes
            for part, (first, out) in enumerate(
                ((0, grad_qk_ref), (features, grad_qk_ref), (0, grad_value_ref))
            ):
                tile = gathered[start + part * lanes : start + (part + 1) * lanes, :]
                out[wide, first + p * lanes : first + (p + 1) * lanes] = tile.T.astype(
                    jnp.float32
                )
            grad_out_ref[p * lanes : (p + 1) * lanes, wide] = gathered[
                start + 3 * lanes : start + 4 * lanes, :
            ].astype(jnp.float32)
    last = gain_sum.shape[0] - 1
    grad_gain_ref[...] = gain_sum[last, 0:1] / gain_ref[...]
    for move in moves[2:]:
        move.start()
    for move in moves:
        move.wait()


F32, BF16 = jnp.float32, jnp.bfloat16
ON_CHIP = pl.BlockSpec(memory_space=pltpu.VMEM)
OFF_CHIP = pl.BlockSpec(memory_space=pltpu.HBM)
SCALARS = pl.BlockSpec(memory_space=pltpu.SMEM)


def attend_call(table, query, d_context, key_value, normed, cot, w_query_key, w_value):
    pairs, pool, _, wide = key_value.shape
    rows, features = cot.shape
    slots = table.shape[1] - 1
    return pl.pallas_call(
        functools.partial(attend_kernel, factor=1.0 / math.sqrt(features // HEADS)),
        out_shape=[
            pltpu.VMEM((pairs, rows, wide // 2), BF16),
            pltpu.VMEM((pairs, rows, wide // 2), BF16),
            pltpu.VMEM((pairs, pool, BLK, wide), BF16),
            pltpu.VMEM((4 * features * (features // LANES), LANES), F32),
            pltpu.VMEM((8, features), F32),
        ],
        in_specs=[SCALARS] + [ON_CHIP] * 7,
        out_specs=[ON_CHIP] * 5,
        scratch_shapes=[
            pltpu.VMEM((pool, BLK, wide), F32),
            pltpu.VMEM((slots * BLK, 2 * BLK), F32),
            pltpu.VMEM((slots * BLK, 2 * BLK), F32),
            pltpu.VMEM((slots * BLK, 2 * BLK), BF16),
            pltpu.VMEM((slots * BLK, 2 * BLK), BF16),
            pltpu.VMEM((BLK, slots * 2 * BLK), BF16),
            pltpu.VMEM((BLK, slots * 2 * BLK), BF16),
        ],
        compiler_params=pltpu.CompilerParams(vmem_limit_bytes=24 << 20),
        name="attend",
    )(table, query, d_context, key_value, normed, cot, w_query_key, w_value)


def shards(
    tokens,
    norm_gain,
    w_query_key,
    w_value,
    w_out,
    cotangent,
    block_order,
    neighbour_ids,
    neighbour_count,
):
    rows, features = tokens.shape[2:]
    blocks = rows // BLK
    slots = neighbour_ids.shape[3] + 1
    extents = (lax.axis_size("bx"), lax.axis_size("by"))
    pairs = HEADS // 2
    lanes = features // pairs
    pool = blocks + 4 * CAP
    gain = norm_gain.reshape(1, features)
    order = block_order.reshape(1, rows)
    ids = neighbour_ids.transpose(1, 2, 3, 0)
    counts = neighbour_count.transpose(1, 2, 0)
    dma = pltpu.SemaphoreType.DMA

    table, sorted_rows, cot, normed, query, d_context, key_value = pl.pallas_call(
        functools.partial(fetch_kernel, extents=extents),
        out_shape=[
            jax.ShapeDtypeStruct((2 * blocks, slots + 1), jnp.int32),
            pltpu.VMEM((blocks, BLK, features), BF16),
            pltpu.VMEM((rows, features), BF16),
            pltpu.VMEM((pool, BLK, features), BF16),
            pltpu.VMEM((pairs, rows, lanes), BF16),
            pltpu.VMEM((pairs, rows, lanes), BF16),
            pltpu.VMEM((pairs, pool, BLK, 2 * lanes), BF16),
        ],
        in_specs=[OFF_CHIP] * 9,
        out_specs=[SCALARS] + [ON_CHIP] * 6,
        scratch_shapes=[
            pltpu.SMEM(ids.shape, jnp.int32),
            pltpu.SMEM(counts.shape, jnp.int32),
            pltpu.VMEM((1, rows), jnp.int32),
            pltpu.VMEM((rows, features), BF16),
            pltpu.VMEM((rows, features), BF16),
            pltpu.VMEM((1, features), F32),
            pltpu.VMEM((features, 2 * features), BF16),
            pltpu.VMEM((features, features), BF16),
            pltpu.VMEM((features, features), BF16),
            pltpu.VMEM((4, CAP, BLK, features), BF16),
            pltpu.VMEM((4, CAP, BLK, features), BF16),
            dma((9,)),
            dma((4,)),
            dma((4,)),
        ],
        compiler_params=pltpu.CompilerParams(
            collective_id=0, has_side_effects=True, vmem_limit_bytes=30 << 20
        ),
        name="fetch",
    )(
        *(
            pltpu.with_memory_space_constraint(operand, pltpu.HBM)
            for operand in (
                ids,
                counts,
                order,
                tokens[0, 0],
                cotangent[0, 0],
                gain,
                w_query_key,
                w_value,
                w_out,
            )
        )
    )
    context, d_query, shipped, grads, gain_part = attend_call(
        table, query, d_context, key_value, normed, cot, w_query_key, w_value
    )

    grad_rows = 4 * features * (features // LANES)
    half = grad_rows // 2
    most = max(extents[0] // 2, extents[1] // 2, 2) - 1
    messages = CHUNKS * (2 + 2 * (extents[0] // 2 + extents[1] // 2 - 1))
    gathered, branch, grad_tokens, gain_sum = pl.pallas_call(
        functools.partial(exchange_kernel, extents=extents),
        out_shape=[
            pltpu.VMEM((grad_rows, LANES), BF16),
            pltpu.VMEM((rows, features), BF16),
            pltpu.VMEM((rows, features), F32),
            pltpu.VMEM((5, 8, features), F32),
        ],
        in_specs=[SCALARS] + [ON_CHIP] * 11,
        out_specs=[ON_CHIP] * 4,
        scratch_shapes=[
            pltpu.VMEM((4, most, 8, features), F32),
            pltpu.VMEM((half, LANES), F32),
            pltpu.VMEM((half, LANES), BF16),
            pltpu.VMEM((half, LANES), BF16),
            pltpu.VMEM((CHUNKS, 2 * half // CHUNKS, LANES), BF16),
            pltpu.VMEM((CHUNKS, 2 * half // CHUNKS, LANES), BF16),
            pltpu.VMEM((4, CAP, BLK, features), BF16),
            pltpu.VMEM((4 * CAP + 1, BLK, features), BF16),
            pltpu.VMEM((rows, features), F32),
            pltpu.VMEM((rows, 2 * features), BF16),
            dma((messages,)),
            dma((messages,)),
            dma((4, most)),
            dma((4, most)),
            dma((4, PIECES)),
            dma((4, PIECES)),
        ],
        compiler_params=pltpu.CompilerParams(
            collective_id=1, has_side_effects=True, vmem_limit_bytes=30 << 20
        ),
        name="exchange",
    )(
        table,
        grads,
        shipped,
        context,
        d_query,
        w_query_key,
        w_value,
        w_out,
        sorted_rows,
        order,
        gain,
        gain_part,
    )

    shape = jax.ShapeDtypeStruct
    grad_qk, grad_value, grad_out, grad_gain, branch, grad_tokens = pl.pallas_call(
        finish_kernel,
        out_shape=[
            shape((features, 2 * features), F32),
            shape((features, features), F32),
            shape((features, features), F32),
            shape((1, features), F32),
            shape((rows, features), BF16),
            shape((rows, features), F32),
        ],
        in_specs=[ON_CHIP] * 5,
        out_specs=[OFF_CHIP] * 3 + [ON_CHIP] + [OFF_CHIP] * 2,
        scratch_shapes=[
            pltpu.VMEM((features, 2 * features), F32),
            pltpu.VMEM((features, features), F32),
            pltpu.VMEM((features, features), F32),
            dma((5,)),
        ],
        compiler_params=pltpu.CompilerParams(vmem_limit_bytes=24 << 20),
        name="finish",
    )(gathered, gain_sum, gain, branch, grad_tokens)
    return (
        branch[None, None],
        grad_tokens[None, None],
        grad_qk,
        grad_value,
        grad_out,
        grad_gain.reshape(features),
    )


def solution(mesh):
    bricks = P("bx", "by", None, None)
    placed = (bricks, P(), P(), P(), P(), bricks, P("bx", "by", None), P(), P())
    return jax.shard_map(
        shards,
        mesh=mesh,
        in_specs=placed,
        out_specs=(bricks, bricks, P(), P(), P(), P()),
        check_vma=False,
    )
```

```python
import functools
import math

import jax
import jax.numpy as jnp
from jax import lax
from jax.experimental import pallas as pl
from jax.experimental.pallas import tpu as pltpu
from jax.sharding import PartitionSpec as P

HEADS = 8
BLK = 256
CAP = 2
LANES = 128
CHUNKS = 4
PIECES = 8
FIRST_PIECES = 2
PACE = 2
EPSILON = 1e-06
MESH = pl.DeviceIdType.MESH
SIDES = ((-1, 0), (1, 0), (0, -1), (0, 1))


def dot(a, b):
    return jnp.dot(a, b, preferred_element_type=jnp.float32)


def dot_nt(a, b):
    return lax.dot_general(a, b, (((1,), (1,)), ((), ())), preferred_element_type=jnp.float32)


def dot_tn(a, b):
    return lax.dot_general(a, b, (((0,), (0,)), ((), ())), preferred_element_type=jnp.float32)


def low(a):
    return a.astype(jnp.bfloat16)


def sides_of(x, y, extents):
    found = []
    for step_x, step_y in SIDES:
        to_x, to_y = x + step_x, y + step_y
        inside = (to_x >= 0) & (to_x < extents[0]) & (to_y >= 0) & (to_y < extents[1])
        found.append(
            (inside, jnp.clip(to_x, 0, extents[0] - 1), jnp.clip(to_y, 0, extents[1] - 1))
        )
    return found


def peers_of(sides):
    return sum(jnp.where(inside, 1, 0) for inside, _, _ in sides)


def wanted_blocks(ids, counts, x, y, inside, first_id, blocks):
    bits = [jnp.int32(0)] * blocks
    for b in range(blocks):
        live = counts[y, b, x]
        for j in range(ids.shape[2]):
            offset = ids[y, b, j, x] - first_id
            hit = inside & (j < live)
            bits = [jnp.where(hit & (offset == o), 1, bits[o]) for o in range(blocks)]
    return bits


def ranks_of(bits):
    ranks, count = [], jnp.int32(0)
    for bit in bits:
        ranks.append(count)
        count = count + bit
    return ranks


def fetch_kernel(
    ids_in,
    counts_in,
    order_in,
    tokens_in,
    cotangent_in,
    gain_in,
    w_qk_in,
    w_value_in,
    w_out_in,
    table_ref,
    sorted_ref,
    cot_ref,
    normed_ref,
    q_ref,
    g_ref,
    kv_ref,
    ids,
    counts,
    order_ref,
    tokens_ref,
    cotangent_ref,
    gain_ref,
    w_qk_ref,
    w_value_ref,
    w_out_ref,
    send,
    recv,
    load_sem,
    send_sem,
    recv_sem,
    *,
    extents,
):
    pairs_of = (
        (order_in, order_ref),
        (tokens_in, tokens_ref),
        (ids_in, ids),
        (counts_in, counts),
        (gain_in, gain_ref),
        (w_qk_in, w_qk_ref),
        (w_value_in, w_value_ref),
        (cotangent_in, cotangent_ref),
        (w_out_in, w_out_ref),
    )
    loads = [
        pltpu.make_async_copy(src, dst, load_sem.at[n]) for n, (src, dst) in enumerate(pairs_of)
    ]
    for load in loads:
        load.start()
    x, y = lax.axis_index("bx"), lax.axis_index("by")
    sides = sides_of(x, y, extents)
    blocks, blk, features = sorted_ref.shape
    rows = blocks * blk
    slots = ids.shape[2]

    barrier = pltpu.get_barrier_semaphore()
    for inside, to_x, to_y in sides:

        @pl.when(inside)
        def _():
            pl.semaphore_signal(barrier, inc=1, device_id=(to_x, to_y), device_id_type=MESH)

    loads[0].wait()
    order = jnp.broadcast_to(order_ref[...].astype(jnp.float32), (LANES, rows)).T
    lane = lax.broadcasted_iota(jnp.int32, (rows, LANES), 1).astype(jnp.float32)
    order_mask = jnp.concatenate(
        [low(jnp.where(order == lane + t * LANES, 1.0, 0.0)) for t in range(rows // LANES)],
        axis=1,
    )
    for load in loads[1:4]:
        load.wait()
    sorted_ref[...] = low(dot(order_mask, tokens_ref[...])).reshape(sorted_ref.shape)

    my_first = (x * extents[1] + y) * blocks
    for s, (inside, to_x, to_y) in enumerate(sides):
        bits = wanted_blocks(ids, counts, to_x, to_y, inside, my_first, blocks)
        ranks = ranks_of(bits)
        for r in range(CAP):
            pick = jnp.int32(0)
            for o in range(blocks):
                pick = jnp.where((bits[o] == 1) & (ranks[o] == r), o, pick)
            send[s, r] = sorted_ref[pick]
        for o in range(blocks):
            table_ref[blocks + o, s] = jnp.where(bits[o] == 1, s * CAP + ranks[o], 4 * CAP)

    copies = []
    for s, (inside, to_x, to_y) in enumerate(sides):
        copies.append(
            pltpu.make_async_remote_copy(
                src_ref=send.at[s],
                dst_ref=recv.at[s ^ 1],
                send_sem=send_sem.at[s],
                recv_sem=recv_sem.at[s ^ 1],
                device_id=(to_x, to_y),
                device_id_type=MESH,
            )
        )
    pl.semaphore_wait(barrier, peers_of(sides))

    for s, (inside, _, _) in enumerate(sides):

        @pl.when(inside)
        def _():
            copies[s].start()

        @pl.when(jnp.logical_not(inside))
        def _():
            recv[s] = jnp.zeros(recv.shape[1:], recv.dtype)

    bits = []
    firsts = []
    for inside, to_x, to_y in sides:
        firsts.append((to_x * extents[1] + to_y) * blocks)
        bits.append(wanted_blocks(ids, counts, x, y, inside, firsts[-1], blocks))
    ranks = [ranks_of(b) for b in bits]
    for b in range(blocks):
        table_ref[b, 0] = jnp.int32(b)
        table_ref[b, slots + 1] = counts[y, b, x]
        for j in range(slots):
            name = ids[y, b, j, x]
            at = name - my_first
            for s, (inside, _, _) in enumerate(sides):
                for o in range(blocks):
                    hit = inside & (name - firsts[s] == o)
                    at = jnp.where(hit, blocks + s * CAP + ranks[s][o], at)
            table_ref[b, j + 1] = at

    for load in loads[4:]:
        load.wait()
    gain = gain_ref[...]
    pairs, lanes = q_ref.shape[0], q_ref.shape[2]

    def project(token_rows, place, count):
        values = token_rows.astype(jnp.float32)
        inv = lax.rsqrt(jnp.mean(values * values, axis=-1, keepdims=True) + EPSILON)
        normed = low(values * inv * gain)
        where = pl.ds(place, count)
        shape = (count, blk, features)
        normed_ref[where] = normed.reshape(shape)
        keys = low(dot(normed, w_qk_ref[:, features:]))
        values = low(dot(normed, w_value_ref[...]))
        for p in range(pairs):
            columns = slice(p * lanes, (p + 1) * lanes)
            kv_ref[p, where, :, :lanes] = keys[:, columns].reshape(count, blk, lanes)
            kv_ref[p, where, :, lanes:] = values[:, columns].reshape(count, blk, lanes)
        return normed

    normed = project(sorted_ref[...].reshape(rows, features), 0, blocks)
    query = low(dot(normed, w_qk_ref[:, :features]))
    cot = low(dot(order_mask, cotangent_ref[...]))
    cot_ref[...] = cot
    grad = low(dot_nt(cot, w_out_ref[...]))
    for p in range(pairs):
        q_ref[p] = query[:, p * lanes : (p + 1) * lanes]
        g_ref[p] = grad[:, p * lanes : (p + 1) * lanes]

    for s in (2, 3, 0, 1):

        @pl.when(sides[s][0])
        def _():
            copies[s ^ 1].wait_recv()

        project(recv[s].reshape(CAP * blk, features), blocks + s * CAP, CAP)
    for s in range(4):

        @pl.when(sides[s][0])
        def _():
            copies[s].wait_send()


def attend_kernel(
    table,
    q_ref,
    g_ref,
    kv_ref,
    normed_ref,
    cot_ref,
    w_qk_ref,
    w_value_ref,
    ctx_ref,
    dq_ref,
    shipped_ref,
    grad_ref,
    gain_ref,
    total,
    scores,
    slopes,
    lows,
    downs,
    turned_p,
    turned_d,
    *,
    factor,
):
    pairs, pool, blk, wide = kv_ref.shape
    rows, features = cot_ref.shape
    lanes = wide // 2
    half = lanes // 2
    blocks = rows // blk
    slots = lows.shape[0] // blk
    lane = lax.broadcasted_iota(jnp.int32, (1, lanes), 1)
    mine = [lane < half, lane >= half]

    def both(a):
        zero = jnp.zeros_like(a)
        return jnp.concatenate([jnp.where(m, a, zero) for m in mine], axis=0)

    def both_t(a):
        zero = jnp.zeros((half, blk), a.dtype)
        return jnp.concatenate(
            [
                jnp.concatenate([a[:half], zero], axis=0),
                jnp.concatenate([zero, a[half:]], axis=0),
            ],
            axis=1,
        )

    def body(pair, block, live):
        here = pl.ds(pl.multiple_of(block * blk, blk), blk)
        query = q_ref[pair, here, :] * jnp.asarray(factor, jnp.bfloat16)
        grad = g_ref[pair, here, :]
        q_cols, g_cols = both_t(query.T), both_t(grad.T)
        q_both, g_both = both(query), both(grad)
        at = [table[block, j] for j in range(live)]

        def part(j):
            return slice(j * blk, (j + 1) * blk)

        top = None
        for j in range(live):
            s_j = dot(kv_ref[pair, at[j], :, :lanes], q_cols)
            scores[part(j), :] = s_j
            m_j = jnp.max(s_j, axis=0, keepdims=True)
            top = m_j if j == 0 else jnp.maximum(top, m_j)
        for j in range(live):
            slope = dot(kv_ref[pair, at[j], :, lanes:], g_cols)
            slopes[part(j), :] = slope
            e_j = jnp.exp(scores[part(j), :] - top)
            scores[part(j), :] = e_j
            n_j = jnp.sum(e_j, axis=0, keepdims=True)
            c_j = jnp.sum(e_j * slope, axis=0, keepdims=True)
            norm = n_j if j == 0 else norm + n_j
            centre = c_j if j == 0 else centre + c_j
        inverse = 1.0 / norm
        centre = centre * inverse
        for j in range(live):
            p_j = scores[part(j), :] * inverse
            low_j = low(p_j)
            d_j = low(p_j * (slopes[part(j), :] - centre))
            lows[part(j), :] = low_j
            downs[part(j), :] = d_j
            for h in range(2):
                columns = slice((2 * j + h) * blk, (2 * j + h + 1) * blk)
                turned_p[:, columns] = low_j[:, h * blk : (h + 1) * blk].T
                turned_d[:, columns] = d_j[:, h * blk : (h + 1) * blk].T
            total[at[j], :, lanes:] += dot(lows[part(j), :], g_both)
            total[at[j], :, :lanes] += dot(downs[part(j), :], q_both)
        span = slice(0, 2 * live * blk)
        v_both = jnp.concatenate([both(kv_ref[pair, a, :, lanes:]) for a in at], axis=0)
        k_both = jnp.concatenate([both(kv_ref[pair, a, :, :lanes]) for a in at], axis=0)
        ctx_ref[pair, here, :] = low(dot(turned_p[:, span], v_both))
        dq_ref[pair, here, :] = low(dot(turned_d[:, span], k_both) * factor)

    width = grad_ref.shape[1]
    span_rows = pairs * 4 * lanes

    def step(pair, _):
        for i in range(pool):
            total[i] = jnp.zeros(total.shape[1:], jnp.float32)

        def inner(block, _):
            count = table[block, slots]
            for live in range(2, slots + 1):
                pl.when(count == live - 1)(functools.partial(body, pair, block, live))
            return 0

        lax.fori_loop(0, blocks, inner, 0)
        shipped_ref[pair] = low(total[...])
        return 0

    lax.fori_loop(0, pairs, step, 0)

    def side_by_side(ref):
        joined = jnp.concatenate([ref[p] for p in range(pairs)], axis=-1)
        return joined.reshape(-1, joined.shape[-1])

    def put(term, size, start):
        for c in range(features // width):
            for p in range(pairs):
                to = c * span_rows + p * 4 * lanes + start
                grad_ref[to : to + size, :] = term[
                    p * size : (p + 1) * size, c * width : (c + 1) * width
                ]

    own = normed_ref[:blocks].reshape(rows, features)
    put(dot_tn(side_by_side(dq_ref), own), lanes, 0)
    put(dot_tn(side_by_side(ctx_ref), cot_ref[...]), lanes, 3 * lanes)
    normed = normed_ref[...].reshape(pool * blk, features)
    put(dot_tn(side_by_side(shipped_ref), normed), wide, lanes)
    for c in range(features // width):
        columns = slice(c * width, (c + 1) * width)
        gain = jnp.zeros((1, width), jnp.float32)
        for p in range(pairs):
            start = c * span_rows + p * 4 * lanes
            for part, (weight, first) in enumerate(
                ((w_qk_ref, 0), (w_qk_ref, features), (w_value_ref, 0))
            ):
                tile = grad_ref[start + part * lanes : start + (part + 1) * lanes, :]
                turned = weight[columns, first + p * lanes : first + (p + 1) * lanes].T
                gain += jnp.sum(tile * turned.astype(jnp.float32), axis=0, keepdims=True)
        gain_ref[:, columns] = jnp.broadcast_to(gain, (gain_ref.shape[0], width))


def exchange_kernel(
    table,
    grad_ref,
    shipped_ref,
    ctx_ref,
    dq_ref,
    w_qk_ref,
    w_value_ref,
    w_out_ref,
    sorted_ref,
    order_ref,
    gain_ref,
    gain_part,
    gathered,
    branch_ref,
    tokens_ref,
    gain_sum,
    gain_in,
    total,
    first_out,
    first_in,
    step_out,
    step_in,
    away,
    back,
    d_normed,
    d_rows,
    send_sem,
    recv_sem,
    gain_send,
    gain_recv,
    back_send,
    back_recv,
    *,
    extents,
):
    x, y = lax.axis_index("bx"), lax.axis_index("by")
    sides = sides_of(x, y, extents)
    blocks, blk, features = sorted_ref.shape
    rows = blocks * blk
    pairs = ctx_ref.shape[0]
    half = grad_ref.shape[0] // 2
    quarter = half // CHUNKS
    core = y % 2
    other_core = (x, y + 1 - 2 * core)
    groups = {
        "y": (extents[1] // 2, y // 2, lambda i: (x, 2 * i + core)),
        "near": (2, x % 2, lambda i: (x // 2 * 2 + i, y)),
        "far": (extents[0] // 2, x // 2, lambda i: (2 * i + x % 2, y)),
    }
    routes = [("y", "far", "near")] * CHUNKS
    sems = iter(range(send_sem.shape[0]))

    def remote(src, dst, to):
        sem = next(sems)
        return pltpu.make_async_remote_copy(
            src_ref=src,
            dst_ref=dst,
            send_sem=send_sem.at[sem],
            recv_sem=recv_sem.at[sem],
            device_id=to,
            device_id_type=MESH,
        )

    barrier = pltpu.get_barrier_semaphore()
    everyone = [other_core]
    for size, index, at in groups.values():
        everyone += [at((index + r) % size) for r in range(1, size)]
    for to in everyone:
        pl.semaphore_signal(barrier, inc=1, device_id=to, device_id_type=MESH)
    for inside, to_x, to_y in sides:

        @pl.when(inside)
        def _():
            pl.semaphore_signal(barrier, inc=1, device_id=(to_x, to_y), device_id_type=MESH)

    base = pl.multiple_of(core * half, half)
    give = pl.multiple_of((1 - core) * half, half)
    first_out[...] = low(grad_ref[pl.ds(give, half), :])
    pl.semaphore_wait(barrier, len(everyone) + peers_of(sides))

    started = []

    def launch(copy):
        copy.start()
        started.append(copy)
        return copy

    firsts = [
        launch(
            remote(
                first_out.at[pl.ds(way * quarter, quarter)],
                first_in.at[pl.ds(way * quarter, quarter)],
                other_core,
            )
        )
        for way in range(CHUNKS)
    ]

    weights = jnp.concatenate(
        [
            piece
            for p in range(pairs)
            for piece in (
                w_qk_ref[:, features + p * LANES : features + (p + 1) * LANES],
                w_value_ref[:, p * LANES : (p + 1) * LANES],
            )
        ],
        axis=1,
    )

    def kv_part(first, count):
        terms = [shipped_ref[p, first : first + count] for p in range(pairs)]
        joined = jnp.concatenate(terms, axis=-1).reshape(count * blk, pairs * 2 * LANES)
        return dot_nt(joined, weights)

    piece_rows = CAP * blk // PIECES
    per_block = PIECES // CAP
    returns = []
    for s, (inside, to_x, to_y) in enumerate(sides):
        returns.append(
            [
                pltpu.make_async_remote_copy(
                    src_ref=away.at[s, k // per_block, pl.ds(k % per_block * piece_rows, piece_rows)],
                    dst_ref=back.at[
                        (s ^ 1) * CAP + k // per_block,
                        pl.ds(k % per_block * piece_rows, piece_rows),
                    ],
                    send_sem=back_send.at[s, k],
                    recv_sem=back_recv.at[s ^ 1, k],
                    device_id=(to_x, to_y),
                    device_id_type=MESH,
                )
                for k in range(PIECES)
            ]
        )

    def make_away(s):
        away[s] = low(kv_part(blocks + s * CAP, CAP)).reshape(CAP, blk, features)

        @pl.when(jnp.logical_not(sides[s][0]))
        def _():
            back[pl.ds(s * CAP, CAP)] = jnp.zeros((CAP, blk, features), back.dtype)

    def send_back(s, first, count):
        @pl.when(sides[s][0])
        def _():
            for k in range(first, first + count):
                returns[s][k].start()

    offsets = [jnp.int32(way * quarter) for way in range(CHUNKS)]
    sizes = [quarter] * CHUNKS
    used = [0] * CHUNKS
    flying = [None] * CHUNKS

    def halve(way, name):
        count, index, at = groups[name]
        piece = sizes[way] // count
        off = pl.multiple_of(offsets[way], sizes[way])
        pos = used[way]
        step_out[way, pl.ds(pos, sizes[way]), :] = low(total[pl.ds(off, sizes[way]), :])
        flying[way] = [
            launch(
                remote(
                    step_out.at[
                        way,
                        pl.ds(pl.multiple_of(pos + (index + r) % count * piece, piece), piece),
                    ],
                    step_in.at[way, pl.ds(pos + r * piece, piece)],
                    at((index + r) % count),
                )
            )
            for r in range(1, count)
        ]

    def settle(way, name):
        count, index, _ = groups[name]
        piece = sizes[way] // count
        for copy in flying[way]:
            copy.wait_recv()
        offsets[way] = offsets[way] + index * piece
        here = pl.ds(pl.multiple_of(offsets[way], piece), piece)
        summed = total[here, :]
        for r in range(1, count):
            summed += step_in[way, pl.ds(used[way] + r * piece, piece), :].astype(jnp.float32)
        used[way] += sizes[way]
        sizes[way] = piece
        return here, summed

    def spread(way, name):
        count, index, at = groups[name]
        where = gathered.at[
            pl.ds(pl.multiple_of(base + offsets[way], sizes[way]), sizes[way])
        ]
        flying[way] = [
            launch(remote(where, where, at((index + r) % count))) for r in range(1, count)
        ]

    def spread_end(way, name):
        count, index, _ = groups[name]
        for copy in flying[way]:
            copy.wait_recv()
        offsets[way] = offsets[way] - index * sizes[way]
        sizes[way] *= count

    lasts = []

    def advance(way, step):
        route = routes[way]
        if step < 3:
            here, summed = settle(way, route[step])
            if step < 2:
                total[here, :] = summed
                halve(way, route[step + 1])
            else:
                to = pl.ds(pl.multiple_of(base + offsets[way], sizes[way]), sizes[way])
                gathered[to, :] = low(summed)
                spread(way, route[2])
        else:
            spread_end(way, route[5 - step])
            if step < 5:
                spread(way, route[4 - step])
            else:
                where = gathered.at[pl.ds(pl.multiple_of(base + way * quarter, quarter), quarter)]
                lasts.append(launch(remote(where, where, other_core)))

    def begin(way):
        halve(way, "y")

    def share(step, name):
        if name == "core":
            peers = [other_core]
        else:
            count, index, at = groups[name]
            peers = [at((index + r) % count) for r in range(1, count)]
        return [
            launch(
                pltpu.make_async_remote_copy(
                    src_ref=gain_sum.at[step],
                    dst_ref=gain_in.at[step, r],
                    send_sem=gain_send.at[step, r],
                    recv_sem=gain_recv.at[step, r],
                    device_id=to,
                    device_id_type=MESH,
                )
            )
            for r, to in enumerate(peers)
        ]

    def shared(step, copies):
        summed = gain_sum[step]
        for r, copy in enumerate(copies):
            copy.wait_recv()
            summed += gain_in[step, r]
        gain_sum[step + 1] = summed

    gain_sum[0] = gain_part[...]
    sharing = share(0, "core")
    make_away(0)
    make_away(1)
    for s in range(2):
        send_back(s, 0, FIRST_PIECES)
    for way in range(CHUNKS):
        firsts[way].wait_recv()
        span = pl.ds(way * quarter, quarter)
        mine = pl.ds(pl.multiple_of(base + way * quarter, quarter), quarter)
        total[span, :] = grad_ref[mine, :] + first_in[span, :].astype(jnp.float32)
        if way < 2:
            begin(way)
    make_away(2)
    make_away(3)
    for s in (2, 3):
        send_back(s, 0, PIECES)
    shared(0, sharing)
    sharing = share(1, "y")
    back[4 * CAP] = jnp.zeros((blk, features), back.dtype)

    order = order_ref[...]

    def unsort(rows_of, i):
        arrival = lax.broadcasted_iota(jnp.int32, (blk, rows), 0) + i * blk
        return dot(low(jnp.where(order == arrival, 1.0, 0.0)), rows_of)

    def own_part():
        d_normed[...] = kv_part(0, blocks)
        query_grad = jnp.concatenate([dq_ref[p] for p in range(pairs)], axis=1)
        d_normed[...] += dot_nt(query_grad, w_qk_ref[:, :features])

    def branch_part():
        context = jnp.concatenate([ctx_ref[p] for p in range(pairs)], axis=1)
        d_rows[:, :features] = low(dot(context, w_out_ref[...]))

    def branch_rows(i):
        branch_ref[i * blk : (i + 1) * blk, :] = low(unsort(d_rows[:, :features], i))

    tasks = [own_part, branch_part] + [
        functools.partial(branch_rows, i) for i in range(blocks)
    ]
    events = sorted(
        ((way, step) for way in range(CHUNKS) for step in range(6)),
        key=lambda e: (e[0] // 2 + e[1], e[0]),
    )
    first_late = next(n for n, e in enumerate(events) if e[0] // 2 + e[1] == 5)
    sent = FIRST_PIECES
    for way, step in events[:first_late]:
        advance(way, step)
        if step == 0 and way + 2 < CHUNKS:
            begin(way + 2)
        if sent < PIECES:
            for s in range(2):
                send_back(s, sent, PACE)
            sent += PACE
        if tasks:
            tasks.pop(0)()
    shared(1, sharing)
    sharing = share(2, "near")
    for task in tasks:
        task()

    for s in range(4):

        @pl.when(sides[s][0])
        def _():
            for k in range(PIECES):
                returns[s ^ 1][k].wait_recv()

    shared(2, sharing)
    sharing = share(3, "far")
    def token_rows(i):
        pieces = unsort(d_rows[...], i)
        tokens_ref[i * blk : (i + 1) * blk, :] = pieces[:, :features] + pieces[:, features:]

    gain = gain_ref[...]
    for o in range(blocks):
        here = slice(o * blk, (o + 1) * blk)
        slope = d_normed[here, :]
        for s in range(4):
            slope = slope + back[table[blocks + o, s]].astype(jnp.float32)
        values = sorted_ref[o].astype(jnp.float32)
        inv = lax.rsqrt(jnp.mean(values * values, axis=-1, keepdims=True) + EPSILON)
        scaled = slope * gain
        inner = jnp.mean(values * scaled, axis=-1, keepdims=True)
        result = inv * scaled - values * ((inv * inv * inv) * inner)
        top = low(result)
        d_rows[here, :features] = top
        d_rows[here, features:] = low(result - top.astype(jnp.float32))

    for n, (way, step) in enumerate(events[first_late:]):
        advance(way, step)
        if n < blocks:
            token_rows(n)
    for n in range(len(events) - first_late, blocks):
        token_rows(n)
    shared(3, sharing)
    for copy in lasts:
        copy.wait_recv()
    for copy in started:
        copy.wait_send()
    for s in range(4):

        @pl.when(sides[s][0])
        def _():
            for k in range(PIECES):
                returns[s][k].wait_send()


def finish_kernel(
    gathered,
    gain_sum,
    gain_ref,
    branch_ref,
    tokens_ref,
    grad_qk_out,
    grad_value_out,
    grad_out_out,
    grad_gain_ref,
    branch_out,
    tokens_out,
    grad_qk_ref,
    grad_value_ref,
    grad_out_ref,
    sem,
):
    moves = [
        pltpu.make_async_copy(src, dst, sem.at[n])
        for n, (src, dst) in enumerate(
            (
                (tokens_ref, tokens_out),
                (branch_ref, branch_out),
                (grad_qk_ref, grad_qk_out),
                (grad_value_ref, grad_value_out),
                (grad_out_ref, grad_out_out),
            )
        )
    ]
    moves[0].start()
    moves[1].start()
    features = grad_out_ref.shape[0]
    width = gathered.shape[1]
    pairs = HEADS // 2
    lanes = features // pairs
    for c in range(features // width):
        wide = slice(c * width, (c + 1) * width)
        for p in range(pairs):
            start = (c * pairs + p) * 4 * lanes
            for part, (first, out) in enumerate(
                ((0, grad_qk_ref), (features, grad_qk_ref), (0, grad_value_ref))
            ):
                tile = gathered[start + part * lanes : start + (part + 1) * lanes, :]
                out[wide, first + p * lanes : first + (p + 1) * lanes] = tile.T.astype(
                    jnp.float32
                )
            grad_out_ref[p * lanes : (p + 1) * lanes, wide] = gathered[
                start + 3 * lanes : start + 4 * lanes, :
            ].astype(jnp.float32)
    last = gain_sum.shape[0] - 1
    grad_gain_ref[...] = gain_sum[last, 0:1] / gain_ref[...]
    for move in moves[2:]:
        move.start()
    for move in moves:
        move.wait()


F32, BF16 = jnp.float32, jnp.bfloat16
ON_CHIP = pl.BlockSpec(memory_space=pltpu.VMEM)
OFF_CHIP = pl.BlockSpec(memory_space=pltpu.HBM)
SCALARS = pl.BlockSpec(memory_space=pltpu.SMEM)


def attend_call(table, query, d_context, key_value, normed, cot, w_query_key, w_value):
    pairs, pool, _, wide = key_value.shape
    rows, features = cot.shape
    slots = table.shape[1] - 1
    return pl.pallas_call(
        functools.partial(attend_kernel, factor=1.0 / math.sqrt(features // HEADS)),
        out_shape=[
            pltpu.VMEM((pairs, rows, wide // 2), BF16),
            pltpu.VMEM((pairs, rows, wide // 2), BF16),
            pltpu.VMEM((pairs, pool, BLK, wide), BF16),
            pltpu.VMEM((4 * features * (features // LANES), LANES), F32),
            pltpu.VMEM((8, features), F32),
        ],
        in_specs=[SCALARS] + [ON_CHIP] * 7,
        out_specs=[ON_CHIP] * 5,
        scratch_shapes=[
            pltpu.VMEM((pool, BLK, wide), F32),
            pltpu.VMEM((slots * BLK, 2 * BLK), F32),
            pltpu.VMEM((slots * BLK, 2 * BLK), F32),
            pltpu.VMEM((slots * BLK, 2 * BLK), BF16),
            pltpu.VMEM((slots * BLK, 2 * BLK), BF16),
            pltpu.VMEM((BLK, slots * 2 * BLK), BF16),
            pltpu.VMEM((BLK, slots * 2 * BLK), BF16),
        ],
        compiler_params=pltpu.CompilerParams(vmem_limit_bytes=24 << 20),
        name="attend",
    )(table, query, d_context, key_value, normed, cot, w_query_key, w_value)


def shards(
    tokens,
    norm_gain,
    w_query_key,
    w_value,
    w_out,
    cotangent,
    block_order,
    neighbour_ids,
    neighbour_count,
):
    rows, features = tokens.shape[2:]
    blocks = rows // BLK
    slots = neighbour_ids.shape[3] + 1
    extents = (lax.axis_size("bx"), lax.axis_size("by"))
    pairs = HEADS // 2
    lanes = features // pairs
    pool = blocks + 4 * CAP
    gain = norm_gain.reshape(1, features)
    order = block_order.reshape(1, rows)
    ids = neighbour_ids.transpose(1, 2, 3, 0)
    counts = neighbour_count.transpose(1, 2, 0)
    dma = pltpu.SemaphoreType.DMA

    table, sorted_rows, cot, normed, query, d_context, key_value = pl.pallas_call(
        functools.partial(fetch_kernel, extents=extents),
        out_shape=[
            jax.ShapeDtypeStruct((2 * blocks, slots + 1), jnp.int32),
            pltpu.VMEM((blocks, BLK, features), BF16),
            pltpu.VMEM((rows, features), BF16),
            pltpu.VMEM((pool, BLK, features), BF16),
            pltpu.VMEM((pairs, rows, lanes), BF16),
            pltpu.VMEM((pairs, rows, lanes), BF16),
            pltpu.VMEM((pairs, pool, BLK, 2 * lanes), BF16),
        ],
        in_specs=[OFF_CHIP] * 9,
        out_specs=[SCALARS] + [ON_CHIP] * 6,
        scratch_shapes=[
            pltpu.SMEM(ids.shape, jnp.int32),
            pltpu.SMEM(counts.shape, jnp.int32),
            pltpu.VMEM((1, rows), jnp.int32),
            pltpu.VMEM((rows, features), BF16),
            pltpu.VMEM((rows, features), BF16),
            pltpu.VMEM((1, features), F32),
            pltpu.VMEM((features, 2 * features), BF16),
            pltpu.VMEM((features, features), BF16),
            pltpu.VMEM((features, features), BF16),
            pltpu.VMEM((4, CAP, BLK, features), BF16),
            pltpu.VMEM((4, CAP, BLK, features), BF16),
            dma((9,)),
            dma((4,)),
            dma((4,)),
        ],
        compiler_params=pltpu.CompilerParams(
            collective_id=0, has_side_effects=True, vmem_limit_bytes=30 << 20
        ),
        name="fetch",
    )(
        *(
            pltpu.with_memory_space_constraint(operand, pltpu.HBM)
            for operand in (
                ids,
                counts,
                order,
                tokens[0, 0],
                cotangent[0, 0],
                gain,
                w_query_key,
                w_value,
                w_out,
            )
        )
    )
    context, d_query, shipped, grads, gain_part = attend_call(
        table, query, d_context, key_value, normed, cot, w_query_key, w_value
    )

    grad_rows = 4 * features * (features // LANES)
    half = grad_rows // 2
    most = max(extents[0] // 2, extents[1] // 2, 2) - 1
    messages = CHUNKS * (2 + 2 * (extents[0] // 2 + extents[1] // 2 - 1))
    gathered, branch, grad_tokens, gain_sum = pl.pallas_call(
        functools.partial(exchange_kernel, extents=extents),
        out_shape=[
            pltpu.VMEM((grad_rows, LANES), BF16),
            pltpu.VMEM((rows, features), BF16),
            pltpu.VMEM((rows, features), F32),
            pltpu.VMEM((5, 8, features), F32),
        ],
        in_specs=[SCALARS] + [ON_CHIP] * 11,
        out_specs=[ON_CHIP] * 4,
        scratch_shapes=[
            pltpu.VMEM((4, most, 8, features), F32),
            pltpu.VMEM((half, LANES), F32),
            pltpu.VMEM((half, LANES), BF16),
            pltpu.VMEM((half, LANES), BF16),
            pltpu.VMEM((CHUNKS, 2 * half // CHUNKS, LANES), BF16),
            pltpu.VMEM((CHUNKS, 2 * half // CHUNKS, LANES), BF16),
            pltpu.VMEM((4, CAP, BLK, features), BF16),
            pltpu.VMEM((4 * CAP + 1, BLK, features), BF16),
            pltpu.VMEM((rows, features), F32),
            pltpu.VMEM((rows, 2 * features), BF16),
            dma((messages,)),
            dma((messages,)),
            dma((4, most)),
            dma((4, most)),
            dma((4, PIECES)),
            dma((4, PIECES)),
        ],
        compiler_params=pltpu.CompilerParams(
            collective_id=1, has_side_effects=True, vmem_limit_bytes=30 << 20
        ),
        name="exchange",
    )(
        table,
        grads,
        shipped,
        context,
        d_query,
        w_query_key,
        w_value,
        w_out,
        sorted_rows,
        order,
        gain,
        gain_part,
    )

    shape = jax.ShapeDtypeStruct
    grad_qk, grad_value, grad_out, grad_gain, branch, grad_tokens = pl.pallas_call(
        finish_kernel,
        out_shape=[
            shape((features, 2 * features), F32),
            shape((features, features), F32),
            shape((features, features), F32),
            shape((1, features), F32),
            shape((rows, features), BF16),
            shape((rows, features), F32),
        ],
        in_specs=[ON_CHIP] * 5,
        out_specs=[OFF_CHIP] * 3 + [ON_CHIP] + [OFF_CHIP] * 2,
        scratch_shapes=[
            pltpu.VMEM((features, 2 * features), F32),
            pltpu.VMEM((features, features), F32),
            pltpu.VMEM((features, features), F32),
            dma((5,)),
        ],
        compiler_params=pltpu.CompilerParams(vmem_limit_bytes=24 << 20),
        name="finish",
    )(gathered, gain_sum, gain, branch, grad_tokens)
    return (
        branch[None, None],
        grad_tokens[None, None],
        grad_qk,
        grad_value,
        grad_out,
        grad_gain.reshape(features),
    )


def solution(mesh):
    bricks = P("bx", "by", None, None)
    placed = (bricks, P(), P(), P(), P(), bricks, P("bx", "by", None), P(), P())
    return jax.shard_map(
        shards,
        mesh=mesh,
        in_specs=placed,
        out_specs=(bricks, bricks, P(), P(), P(), P()),
        check_vma=False,
    )
```

```python
import functools
import math

import jax
import jax.numpy as jnp
from jax import lax
from jax.experimental import pallas as pl
from jax.experimental.pallas import tpu as pltpu
from jax.sharding import PartitionSpec as P

HEADS = 8
BLK = 256
CAP = 2
LANES = 128
CHUNKS = 4
PIECES = 8
FIRST_PIECES = 2
PACE = 2
EPSILON = 1e-06
MESH = pl.DeviceIdType.MESH
SIDES = ((-1, 0), (1, 0), (0, -1), (0, 1))


def dot(a, b):
    return jnp.dot(a, b, preferred_element_type=jnp.float32)


def dot_nt(a, b):
    return lax.dot_general(a, b, (((1,), (1,)), ((), ())), preferred_element_type=jnp.float32)


def dot_tn(a, b):
    return lax.dot_general(a, b, (((0,), (0,)), ((), ())), preferred_element_type=jnp.float32)


def low(a):
    return a.astype(jnp.bfloat16)


def sides_of(x, y, extents):
    found = []
    for step_x, step_y in SIDES:
        to_x, to_y = x + step_x, y + step_y
        inside = (to_x >= 0) & (to_x < extents[0]) & (to_y >= 0) & (to_y < extents[1])
        found.append(
            (inside, jnp.clip(to_x, 0, extents[0] - 1), jnp.clip(to_y, 0, extents[1] - 1))
        )
    return found


def peers_of(sides):
    return sum(jnp.where(inside, 1, 0) for inside, _, _ in sides)


def wanted_blocks(ids, counts, x, y, inside, first_id, blocks):
    bits = [jnp.int32(0)] * blocks
    for b in range(blocks):
        live = counts[y, b, x]
        for j in range(ids.shape[2]):
            offset = ids[y, b, j, x] - first_id
            hit = inside & (j < live)
            bits = [jnp.where(hit & (offset == o), 1, bits[o]) for o in range(blocks)]
    return bits


def ranks_of(bits):
    ranks, count = [], jnp.int32(0)
    for bit in bits:
        ranks.append(count)
        count = count + bit
    return ranks


def fetch_kernel(
    ids_in,
    counts_in,
    order_in,
    tokens_in,
    cotangent_in,
    gain_in,
    w_qk_in,
    w_value_in,
    w_out_in,
    table_ref,
    sorted_ref,
    cot_ref,
    normed_ref,
    q_ref,
    g_ref,
    kv_ref,
    ids,
    counts,
    order_ref,
    tokens_ref,
    cotangent_ref,
    gain_ref,
    w_qk_ref,
    w_value_ref,
    w_out_ref,
    send,
    recv,
    load_sem,
    send_sem,
    recv_sem,
    *,
    extents,
):
    pairs_of = (
        (order_in, order_ref),
        (tokens_in, tokens_ref),
        (ids_in, ids),
        (counts_in, counts),
        (gain_in, gain_ref),
        (w_qk_in, w_qk_ref),
        (w_value_in, w_value_ref),
        (cotangent_in, cotangent_ref),
        (w_out_in, w_out_ref),
    )
    loads = [
        pltpu.make_async_copy(src, dst, load_sem.at[n]) for n, (src, dst) in enumerate(pairs_of)
    ]
    for load in loads:
        load.start()
    x, y = lax.axis_index("bx"), lax.axis_index("by")
    sides = sides_of(x, y, extents)
    blocks, blk, features = sorted_ref.shape
    rows = blocks * blk
    slots = ids.shape[2]

    barrier = pltpu.get_barrier_semaphore()
    for inside, to_x, to_y in sides:

        @pl.when(inside)
        def _():
            pl.semaphore_signal(barrier, inc=1, device_id=(to_x, to_y), device_id_type=MESH)

    loads[0].wait()
    order = jnp.broadcast_to(order_ref[...].astype(jnp.float32), (LANES, rows)).T
    lane = lax.broadcasted_iota(jnp.int32, (rows, LANES), 1).astype(jnp.float32)
    order_mask = jnp.concatenate(
        [low(jnp.where(order == lane + t * LANES, 1.0, 0.0)) for t in range(rows // LANES)],
        axis=1,
    )
    for load in loads[1:4]:
        load.wait()
    sorted_ref[...] = low(dot(order_mask, tokens_ref[...])).reshape(sorted_ref.shape)

    my_first = (x * extents[1] + y) * blocks
    for s, (inside, to_x, to_y) in enumerate(sides):
        bits = wanted_blocks(ids, counts, to_x, to_y, inside, my_first, blocks)
        ranks = ranks_of(bits)
        for r in range(CAP):
            pick = jnp.int32(0)
            for o in range(blocks):
                pick = jnp.where((bits[o] == 1) & (ranks[o] == r), o, pick)
            send[s, r] = sorted_ref[pick]
        for o in range(blocks):
            table_ref[blocks + o, s] = jnp.where(bits[o] == 1, s * CAP + ranks[o], 4 * CAP)

    copies = []
    for s, (inside, to_x, to_y) in enumerate(sides):
        copies.append(
            pltpu.make_async_remote_copy(
                src_ref=send.at[s],
                dst_ref=recv.at[s ^ 1],
                send_sem=send_sem.at[s],
                recv_sem=recv_sem.at[s ^ 1],
                device_id=(to_x, to_y),
                device_id_type=MESH,
            )
        )
    pl.semaphore_wait(barrier, peers_of(sides))

    for s, (inside, _, _) in enumerate(sides):

        @pl.when(inside)
        def _():
            copies[s].start()

        @pl.when(jnp.logical_not(inside))
        def _():
            recv[s] = jnp.zeros(recv.shape[1:], recv.dtype)

    bits = []
    firsts = []
    for inside, to_x, to_y in sides:
        firsts.append((to_x * extents[1] + to_y) * blocks)
        bits.append(wanted_blocks(ids, counts, x, y, inside, firsts[-1], blocks))
    ranks = [ranks_of(b) for b in bits]
    for b in range(blocks):
        table_ref[b, 0] = jnp.int32(b)
        table_ref[b, slots + 1] = counts[y, b, x]
        for j in range(slots):
            name = ids[y, b, j, x]
            at = name - my_first
            for s, (inside, _, _) in enumerate(sides):
                for o in range(blocks):
                    hit = inside & (name - firsts[s] == o)
                    at = jnp.where(hit, blocks + s * CAP + ranks[s][o], at)
            table_ref[b, j + 1] = at

    for load in loads[4:]:
        load.wait()
    gain = gain_ref[...]
    pairs, lanes = q_ref.shape[0], q_ref.shape[2]

    def project(token_rows, place, count):
        values = token_rows.astype(jnp.float32)
        inv = lax.rsqrt(jnp.mean(values * values, axis=-1, keepdims=True) + EPSILON)
        normed = low(values * inv * gain)
        where = pl.ds(place, count)
        shape = (count, blk, features)
        normed_ref[where] = normed.reshape(shape)
        keys = low(dot(normed, w_qk_ref[:, features:]))
        values = low(dot(normed, w_value_ref[...]))
        for p in range(pairs):
            columns = slice(p * lanes, (p + 1) * lanes)
            kv_ref[p, where, :, :lanes] = keys[:, columns].reshape(count, blk, lanes)
            kv_ref[p, where, :, lanes:] = values[:, columns].reshape(count, blk, lanes)
        return normed

    normed = project(sorted_ref[...].reshape(rows, features), 0, blocks)
    query = low(dot(normed, w_qk_ref[:, :features]))
    cot = low(dot(order_mask, cotangent_ref[...]))
    cot_ref[...] = cot
    grad = low(dot_nt(cot, w_out_ref[...]))
    for p in range(pairs):
        q_ref[p] = query[:, p * lanes : (p + 1) * lanes]
        g_ref[p] = grad[:, p * lanes : (p + 1) * lanes]

    for s in (2, 3, 0, 1):

        @pl.when(sides[s][0])
        def _():
            copies[s ^ 1].wait_recv()

        project(recv[s].reshape(CAP * blk, features), blocks + s * CAP, CAP)
    for s in range(4):

        @pl.when(sides[s][0])
        def _():
            copies[s].wait_send()


def attend_kernel(
    table,
    q_ref,
    g_ref,
    kv_ref,
    normed_ref,
    cot_ref,
    w_qk_ref,
    w_value_ref,
    ctx_ref,
    dq_ref,
    shipped_ref,
    grad_ref,
    gain_ref,
    total,
    scores,
    slopes,
    lows,
    downs,
    turned_p,
    turned_d,
    *,
    factor,
):
    pairs, pool, blk, wide = kv_ref.shape
    rows, features = cot_ref.shape
    lanes = wide // 2
    half = lanes // 2
    blocks = rows // blk
    slots = lows.shape[0] // blk
    lane = lax.broadcasted_iota(jnp.int32, (1, lanes), 1)
    mine = [lane < half, lane >= half]

    def both(a):
        zero = jnp.zeros_like(a)
        return jnp.concatenate([jnp.where(m, a, zero) for m in mine], axis=0)

    def both_t(a):
        zero = jnp.zeros((half, blk), a.dtype)
        return jnp.concatenate(
            [
                jnp.concatenate([a[:half], zero], axis=0),
                jnp.concatenate([zero, a[half:]], axis=0),
            ],
            axis=1,
        )

    def body(pair, block, live):
        here = pl.ds(pl.multiple_of(block * blk, blk), blk)
        query = q_ref[pair, here, :] * jnp.asarray(factor, jnp.bfloat16)
        grad = g_ref[pair, here, :]
        q_cols, g_cols = both_t(query.T), both_t(grad.T)
        q_both, g_both = both(query), both(grad)
        at = [table[block, j] for j in range(live)]

        def part(j):
            return slice(j * blk, (j + 1) * blk)

        top = None
        for j in range(live):
            s_j = dot(kv_ref[pair, at[j], :, :lanes], q_cols)
            scores[part(j), :] = s_j
            m_j = jnp.max(s_j, axis=0, keepdims=True)
            top = m_j if j == 0 else jnp.maximum(top, m_j)
        for j in range(live):
            slope = dot(kv_ref[pair, at[j], :, lanes:], g_cols)
            slopes[part(j), :] = slope
            e_j = jnp.exp(scores[part(j), :] - top)
            scores[part(j), :] = e_j
            n_j = jnp.sum(e_j, axis=0, keepdims=True)
            c_j = jnp.sum(e_j * slope, axis=0, keepdims=True)
            norm = n_j if j == 0 else norm + n_j
            centre = c_j if j == 0 else centre + c_j
        inverse = 1.0 / norm
        centre = centre * inverse
        for j in range(live):
            p_j = scores[part(j), :] * inverse
            low_j = low(p_j)
            d_j = low(p_j * (slopes[part(j), :] - centre))
            lows[part(j), :] = low_j
            downs[part(j), :] = d_j
            for h in range(2):
                columns = slice((2 * j + h) * blk, (2 * j + h + 1) * blk)
                turned_p[:, columns] = low_j[:, h * blk : (h + 1) * blk].T
                turned_d[:, columns] = d_j[:, h * blk : (h + 1) * blk].T
            total[at[j], :, lanes:] += dot(lows[part(j), :], g_both)
            total[at[j], :, :lanes] += dot(downs[part(j), :], q_both)
        span = slice(0, 2 * live * blk)
        v_both = jnp.concatenate([both(kv_ref[pair, a, :, lanes:]) for a in at], axis=0)
        k_both = jnp.concatenate([both(kv_ref[pair, a, :, :lanes]) for a in at], axis=0)
        ctx_ref[pair, here, :] = low(dot(turned_p[:, span], v_both))
        dq_ref[pair, here, :] = low(dot(turned_d[:, span], k_both) * factor)

    width = grad_ref.shape[1]
    span_rows = pairs * 4 * lanes

    def step(pair, _):
        for i in range(pool):
            total[i] = jnp.zeros(total.shape[1:], jnp.float32)

        def inner(block, _):
            count = table[block, slots]
            for live in range(2, slots + 1):
                pl.when(count == live - 1)(functools.partial(body, pair, block, live))
            return 0

        lax.fori_loop(0, blocks, inner, 0)
        shipped_ref[pair] = low(total[...])
        return 0

    lax.fori_loop(0, pairs, step, 0)

    def side_by_side(ref):
        joined = jnp.concatenate([ref[p] for p in range(pairs)], axis=-1)
        return joined.reshape(-1, joined.shape[-1])

    def put(term, size, start):
        for c in range(features // width):
            for p in range(pairs):
                to = c * span_rows + p * 4 * lanes + start
                grad_ref[to : to + size, :] = term[
                    p * size : (p + 1) * size, c * width : (c + 1) * width
                ]

    own = normed_ref[:blocks].reshape(rows, features)
    put(dot_tn(side_by_side(dq_ref), own), lanes, 0)
    put(dot_tn(side_by_side(ctx_ref), cot_ref[...]), lanes, 3 * lanes)
    normed = normed_ref[...].reshape(pool * blk, features)
    put(dot_tn(side_by_side(shipped_ref), normed), wide, lanes)
    for c in range(features // width):
        columns = slice(c * width, (c + 1) * width)
        gain = jnp.zeros((1, width), jnp.float32)
        for p in range(pairs):
            start = c * span_rows + p * 4 * lanes
            for part, (weight, first) in enumerate(
                ((w_qk_ref, 0), (w_qk_ref, features), (w_value_ref, 0))
            ):
                tile = grad_ref[start + part * lanes : start + (part + 1) * lanes, :]
                turned = weight[columns, first + p * lanes : first + (p + 1) * lanes].T
                gain += jnp.sum(tile * turned.astype(jnp.float32), axis=0, keepdims=True)
        gain_ref[:, columns] = jnp.broadcast_to(gain, (gain_ref.shape[0], width))


def exchange_kernel(
    table,
    grad_ref,
    shipped_ref,
    ctx_ref,
    dq_ref,
    w_qk_ref,
    w_value_ref,
    w_out_ref,
    sorted_ref,
    order_ref,
    gain_ref,
    gain_part,
    gathered,
    branch_ref,
    tokens_ref,
    gain_sum,
    gain_in,
    total,
    first_out,
    first_in,
    step_out,
    step_in,
    away,
    back,
    d_normed,
    d_rows,
    send_sem,
    recv_sem,
    gain_send,
    gain_recv,
    back_send,
    back_recv,
    *,
    extents,
):
    x, y = lax.axis_index("bx"), lax.axis_index("by")
    sides = sides_of(x, y, extents)
    blocks, blk, features = sorted_ref.shape
    rows = blocks * blk
    pairs = ctx_ref.shape[0]
    half = grad_ref.shape[0] // 2
    quarter = half // CHUNKS
    core = y % 2
    other_core = (x, y + 1 - 2 * core)
    groups = {
        "y": (extents[1] // 2, y // 2, lambda i: (x, 2 * i + core)),
        "near": (2, x % 2, lambda i: (x // 2 * 2 + i, y)),
        "far": (extents[0] // 2, x // 2, lambda i: (2 * i + x % 2, y)),
    }
    routes = [("y", "far", "near")] * CHUNKS
    sems = iter(range(send_sem.shape[0]))

    def remote(src, dst, to):
        sem = next(sems)
        return pltpu.make_async_remote_copy(
            src_ref=src,
            dst_ref=dst,
            send_sem=send_sem.at[sem],
            recv_sem=recv_sem.at[sem],
            device_id=to,
            device_id_type=MESH,
        )

    barrier = pltpu.get_barrier_semaphore()
    everyone = [other_core]
    for size, index, at in groups.values():
        everyone += [at((index + r) % size) for r in range(1, size)]
    for to in everyone:
        pl.semaphore_signal(barrier, inc=1, device_id=to, device_id_type=MESH)
    for inside, to_x, to_y in sides:

        @pl.when(inside)
        def _():
            pl.semaphore_signal(barrier, inc=1, device_id=(to_x, to_y), device_id_type=MESH)

    base = pl.multiple_of(core * half, half)
    give = pl.multiple_of((1 - core) * half, half)
    first_out[...] = low(grad_ref[pl.ds(give, half), :])
    pl.semaphore_wait(barrier, len(everyone) + peers_of(sides))

    started = []

    def launch(copy):
        copy.start()
        started.append(copy)
        return copy

    firsts = [
        launch(
            remote(
                first_out.at[pl.ds(way * quarter, quarter)],
                first_in.at[pl.ds(way * quarter, quarter)],
                other_core,
            )
        )
        for way in range(CHUNKS)
    ]

    weights = jnp.concatenate(
        [
            piece
            for p in range(pairs)
            for piece in (
                w_qk_ref[:, features + p * LANES : features + (p + 1) * LANES],
                w_value_ref[:, p * LANES : (p + 1) * LANES],
            )
        ],
        axis=1,
    )

    def kv_part(first, count):
        terms = [shipped_ref[p, first : first + count] for p in range(pairs)]
        joined = jnp.concatenate(terms, axis=-1).reshape(count * blk, pairs * 2 * LANES)
        return dot_nt(joined, weights)

    piece_rows = CAP * blk // PIECES
    per_block = PIECES // CAP
    returns = []
    for s, (inside, to_x, to_y) in enumerate(sides):
        returns.append(
            [
                pltpu.make_async_remote_copy(
                    src_ref=away.at[s, k // per_block, pl.ds(k % per_block * piece_rows, piece_rows)],
                    dst_ref=back.at[
                        (s ^ 1) * CAP + k // per_block,
                        pl.ds(k % per_block * piece_rows, piece_rows),
                    ],
                    send_sem=back_send.at[s, k],
                    recv_sem=back_recv.at[s ^ 1, k],
                    device_id=(to_x, to_y),
                    device_id_type=MESH,
                )
                for k in range(PIECES)
            ]
        )

    def make_away(s):
        away[s] = low(kv_part(blocks + s * CAP, CAP)).reshape(CAP, blk, features)

        @pl.when(jnp.logical_not(sides[s][0]))
        def _():
            back[pl.ds(s * CAP, CAP)] = jnp.zeros((CAP, blk, features), back.dtype)

    def send_back(s, first, count):
        @pl.when(sides[s][0])
        def _():
            for k in range(first, first + count):
                returns[s][k].start()

    offsets = [jnp.int32(way * quarter) for way in range(CHUNKS)]
    sizes = [quarter] * CHUNKS
    used = [0] * CHUNKS
    flying = [None] * CHUNKS

    def halve(way, name):
        count, index, at = groups[name]
        piece = sizes[way] // count
        off = pl.multiple_of(offsets[way], sizes[way])
        pos = used[way]
        step_out[way, pl.ds(pos, sizes[way]), :] = low(total[pl.ds(off, sizes[way]), :])
        flying[way] = [
            launch(
                remote(
                    step_out.at[
                        way,
                        pl.ds(pl.multiple_of(pos + (index + r) % count * piece, piece), piece),
                    ],
                    step_in.at[way, pl.ds(pos + r * piece, piece)],
                    at((index + r) % count),
                )
            )
            for r in range(1, count)
        ]

    def settle(way, name):
        count, index, _ = groups[name]
        piece = sizes[way] // count
        for copy in flying[way]:
            copy.wait_recv()
        offsets[way] = offsets[way] + index * piece
        here = pl.ds(pl.multiple_of(offsets[way], piece), piece)
        summed = total[here, :]
        for r in range(1, count):
            summed += step_in[way, pl.ds(used[way] + r * piece, piece), :].astype(jnp.float32)
        used[way] += sizes[way]
        sizes[way] = piece
        return here, summed

    def spread(way, name):
        count, index, at = groups[name]
        where = gathered.at[
            pl.ds(pl.multiple_of(base + offsets[way], sizes[way]), sizes[way])
        ]
        flying[way] = [
            launch(remote(where, where, at((index + r) % count))) for r in range(1, count)
        ]

    def spread_end(way, name):
        count, index, _ = groups[name]
        for copy in flying[way]:
            copy.wait_recv()
        offsets[way] = offsets[way] - index * sizes[way]
        sizes[way] *= count

    lasts = []

    def advance(way, step):
        route = routes[way]
        if step < 3:
            here, summed = settle(way, route[step])
            if step < 2:
                total[here, :] = summed
                halve(way, route[step + 1])
            else:
                to = pl.ds(pl.multiple_of(base + offsets[way], sizes[way]), sizes[way])
                gathered[to, :] = low(summed)
                spread(way, route[2])
        else:
            spread_end(way, route[5 - step])
            if step < 5:
                spread(way, route[4 - step])
            else:
                where = gathered.at[pl.ds(pl.multiple_of(base + way * quarter, quarter), quarter)]
                lasts.append(launch(remote(where, where, other_core)))

    def begin(way):
        halve(way, "y")

    def share(step, name):
        if name == "core":
            peers = [other_core]
        else:
            count, index, at = groups[name]
            peers = [at((index + r) % count) for r in range(1, count)]
        return [
            launch(
                pltpu.make_async_remote_copy(
                    src_ref=gain_sum.at[step],
                    dst_ref=gain_in.at[step, r],
                    send_sem=gain_send.at[step, r],
                    recv_sem=gain_recv.at[step, r],
                    device_id=to,
                    device_id_type=MESH,
                )
            )
            for r, to in enumerate(peers)
        ]

    def shared(step, copies):
        summed = gain_sum[step]
        for r, copy in enumerate(copies):
            copy.wait_recv()
            summed += gain_in[step, r]
        gain_sum[step + 1] = summed

    gain_sum[0] = gain_part[...]
    sharing = share(0, "core")
    make_away(0)
    make_away(1)
    for s in range(2):
        send_back(s, 0, FIRST_PIECES)
    for way in range(CHUNKS):
        firsts[way].wait_recv()
        span = pl.ds(way * quarter, quarter)
        mine = pl.ds(pl.multiple_of(base + way * quarter, quarter), quarter)
        total[span, :] = grad_ref[mine, :] + first_in[span, :].astype(jnp.float32)
        begin(way)
    make_away(2)
    make_away(3)
    for s in (2, 3):
        send_back(s, 0, PIECES)
    shared(0, sharing)
    sharing = share(1, "y")
    back[4 * CAP] = jnp.zeros((blk, features), back.dtype)

    order = order_ref[...]

    def unsort(rows_of, i):
        arrival = lax.broadcasted_iota(jnp.int32, (blk, rows), 0) + i * blk
        return dot(low(jnp.where(order == arrival, 1.0, 0.0)), rows_of)

    def own_part():
        d_normed[...] = kv_part(0, blocks)
        query_grad = jnp.concatenate([dq_ref[p] for p in range(pairs)], axis=1)
        d_normed[...] += dot_nt(query_grad, w_qk_ref[:, :features])

    def branch_part():
        context = jnp.concatenate([ctx_ref[p] for p in range(pairs)], axis=1)
        d_rows[:, :features] = low(dot(context, w_out_ref[...]))

    def branch_rows(i):
        branch_ref[i * blk : (i + 1) * blk, :] = low(unsort(d_rows[:, :features], i))

    own_part()
    tasks = [branch_part] + [
        functools.partial(branch_rows, i) for i in range(blocks)
    ]
    events = sorted(
        ((way, step) for way in range(CHUNKS) for step in range(6)),
        key=lambda e: (e[0] // 2 + e[1], e[0]),
    )
    first_late = next(n for n, e in enumerate(events) if e[0] // 2 + e[1] == 5)
    sent = FIRST_PIECES
    for way, step in events[:first_late]:
        advance(way, step)
        if sent < PIECES:
            for s in range(2):
                send_back(s, sent, PACE)
            sent += PACE
        if tasks:
            tasks.pop(0)()
    shared(1, sharing)
    sharing = share(2, "near")
    for task in tasks:
        task()

    for s in range(4):

        @pl.when(sides[s][0])
        def _():
            for k in range(PIECES):
                returns[s ^ 1][k].wait_recv()

    shared(2, sharing)
    sharing = share(3, "far")
    def token_rows(i):
        pieces = unsort(d_rows[...], i)
        tokens_ref[i * blk : (i + 1) * blk, :] = pieces[:, :features] + pieces[:, features:]

    gain = gain_ref[...]
    for o in range(blocks):
        here = slice(o * blk, (o + 1) * blk)
        slope = d_normed[here, :]
        for s in range(4):
            slope = slope + back[table[blocks + o, s]].astype(jnp.float32)
        values = sorted_ref[o].astype(jnp.float32)
        inv = lax.rsqrt(jnp.mean(values * values, axis=-1, keepdims=True) + EPSILON)
        scaled = slope * gain
        inner = jnp.mean(values * scaled, axis=-1, keepdims=True)
        result = inv * scaled - values * ((inv * inv * inv) * inner)
        top = low(result)
        d_rows[here, :features] = top
        d_rows[here, features:] = low(result - top.astype(jnp.float32))

    for n, (way, step) in enumerate(events[first_late:]):
        advance(way, step)
        if n < blocks:
            token_rows(n)
    for n in range(len(events) - first_late, blocks):
        token_rows(n)
    shared(3, sharing)
    for copy in lasts:
        copy.wait_recv()
    for copy in started:
        copy.wait_send()
    for s in range(4):

        @pl.when(sides[s][0])
        def _():
            for k in range(PIECES):
                returns[s][k].wait_send()


def finish_kernel(
    gathered,
    gain_sum,
    gain_ref,
    branch_ref,
    tokens_ref,
    grad_qk_out,
    grad_value_out,
    grad_out_out,
    grad_gain_ref,
    branch_out,
    tokens_out,
    grad_qk_ref,
    grad_value_ref,
    grad_out_ref,
    sem,
):
    moves = [
        pltpu.make_async_copy(src, dst, sem.at[n])
        for n, (src, dst) in enumerate(
            (
                (tokens_ref, tokens_out),
                (branch_ref, branch_out),
                (grad_qk_ref, grad_qk_out),
                (grad_value_ref, grad_value_out),
                (grad_out_ref, grad_out_out),
            )
        )
    ]
    moves[0].start()
    moves[1].start()
    features = grad_out_ref.shape[0]
    width = gathered.shape[1]
    pairs = HEADS // 2
    lanes = features // pairs
    for c in range(features // width):
        wide = slice(c * width, (c + 1) * width)
        for p in range(pairs):
            start = (c * pairs + p) * 4 * lanes
            for part, (first, out) in enumerate(
                ((0, grad_qk_ref), (features, grad_qk_ref), (0, grad_value_ref))
            ):
                tile = gathered[start + part * lanes : start + (part + 1) * lanes, :]
                out[wide, first + p * lanes : first + (p + 1) * lanes] = tile.T.astype(
                    jnp.float32
                )
            grad_out_ref[p * lanes : (p + 1) * lanes, wide] = gathered[
                start + 3 * lanes : start + 4 * lanes, :
            ].astype(jnp.float32)
    last = gain_sum.shape[0] - 1
    grad_gain_ref[...] = gain_sum[last, 0:1] / gain_ref[...]
    for move in moves[2:]:
        move.start()
    for move in moves:
        move.wait()


F32, BF16 = jnp.float32, jnp.bfloat16
ON_CHIP = pl.BlockSpec(memory_space=pltpu.VMEM)
OFF_CHIP = pl.BlockSpec(memory_space=pltpu.HBM)
SCALARS = pl.BlockSpec(memory_space=pltpu.SMEM)


def attend_call(table, query, d_context, key_value, normed, cot, w_query_key, w_value):
    pairs, pool, _, wide = key_value.shape
    rows, features = cot.shape
    slots = table.shape[1] - 1
    return pl.pallas_call(
        functools.partial(attend_kernel, factor=1.0 / math.sqrt(features // HEADS)),
        out_shape=[
            pltpu.VMEM((pairs, rows, wide // 2), BF16),
            pltpu.VMEM((pairs, rows, wide // 2), BF16),
            pltpu.VMEM((pairs, pool, BLK, wide), BF16),
            pltpu.VMEM((4 * features * (features // LANES), LANES), F32),
            pltpu.VMEM((8, features), F32),
        ],
        in_specs=[SCALARS] + [ON_CHIP] * 7,
        out_specs=[ON_CHIP] * 5,
        scratch_shapes=[
            pltpu.VMEM((pool, BLK, wide), F32),
            pltpu.VMEM((slots * BLK, 2 * BLK), F32),
            pltpu.VMEM((slots * BLK, 2 * BLK), F32),
            pltpu.VMEM((slots * BLK, 2 * BLK), BF16),
            pltpu.VMEM((slots * BLK, 2 * BLK), BF16),
            pltpu.VMEM((BLK, slots * 2 * BLK), BF16),
            pltpu.VMEM((BLK, slots * 2 * BLK), BF16),
        ],
        compiler_params=pltpu.CompilerParams(vmem_limit_bytes=24 << 20),
        name="attend",
    )(table, query, d_context, key_value, normed, cot, w_query_key, w_value)


def shards(
    tokens,
    norm_gain,
    w_query_key,
    w_value,
    w_out,
    cotangent,
    block_order,
    neighbour_ids,
    neighbour_count,
):
    rows, features = tokens.shape[2:]
    blocks = rows // BLK
    slots = neighbour_ids.shape[3] + 1
    extents = (lax.axis_size("bx"), lax.axis_size("by"))
    pairs = HEADS // 2
    lanes = features // pairs
    pool = blocks + 4 * CAP
    gain = norm_gain.reshape(1, features)
    order = block_order.reshape(1, rows)
    ids = neighbour_ids.transpose(1, 2, 3, 0)
    counts = neighbour_count.transpose(1, 2, 0)
    dma = pltpu.SemaphoreType.DMA

    table, sorted_rows, cot, normed, query, d_context, key_value = pl.pallas_call(
        functools.partial(fetch_kernel, extents=extents),
        out_shape=[
            jax.ShapeDtypeStruct((2 * blocks, slots + 1), jnp.int32),
            pltpu.VMEM((blocks, BLK, features), BF16),
            pltpu.VMEM((rows, features), BF16),
            pltpu.VMEM((pool, BLK, features), BF16),
            pltpu.VMEM((pairs, rows, lanes), BF16),
            pltpu.VMEM((pairs, rows, lanes), BF16),
            pltpu.VMEM((pairs, pool, BLK, 2 * lanes), BF16),
        ],
        in_specs=[OFF_CHIP] * 9,
        out_specs=[SCALARS] + [ON_CHIP] * 6,
        scratch_shapes=[
            pltpu.SMEM(ids.shape, jnp.int32),
            pltpu.SMEM(counts.shape, jnp.int32),
            pltpu.VMEM((1, rows), jnp.int32),
            pltpu.VMEM((rows, features), BF16),
            pltpu.VMEM((rows, features), BF16),
            pltpu.VMEM((1, features), F32),
            pltpu.VMEM((features, 2 * features), BF16),
            pltpu.VMEM((features, features), BF16),
            pltpu.VMEM((features, features), BF16),
            pltpu.VMEM((4, CAP, BLK, features), BF16),
            pltpu.VMEM((4, CAP, BLK, features), BF16),
            dma((9,)),
            dma((4,)),
            dma((4,)),
        ],
        compiler_params=pltpu.CompilerParams(
            collective_id=0, has_side_effects=True, vmem_limit_bytes=30 << 20
        ),
        name="fetch",
    )(
        *(
            pltpu.with_memory_space_constraint(operand, pltpu.HBM)
            for operand in (
                ids,
                counts,
                order,
                tokens[0, 0],
                cotangent[0, 0],
                gain,
                w_query_key,
                w_value,
                w_out,
            )
        )
    )
    context, d_query, shipped, grads, gain_part = attend_call(
        table, query, d_context, key_value, normed, cot, w_query_key, w_value
    )

    grad_rows = 4 * features * (features // LANES)
    half = grad_rows // 2
    most = max(extents[0] // 2, extents[1] // 2, 2) - 1
    messages = CHUNKS * (2 + 2 * (extents[0] // 2 + extents[1] // 2 - 1))
    gathered, branch, grad_tokens, gain_sum = pl.pallas_call(
        functools.partial(exchange_kernel, extents=extents),
        out_shape=[
            pltpu.VMEM((grad_rows, LANES), BF16),
            pltpu.VMEM((rows, features), BF16),
            pltpu.VMEM((rows, features), F32),
            pltpu.VMEM((5, 8, features), F32),
        ],
        in_specs=[SCALARS] + [ON_CHIP] * 11,
        out_specs=[ON_CHIP] * 4,
        scratch_shapes=[
            pltpu.VMEM((4, most, 8, features), F32),
            pltpu.VMEM((half, LANES), F32),
            pltpu.VMEM((half, LANES), BF16),
            pltpu.VMEM((half, LANES), BF16),
            pltpu.VMEM((CHUNKS, 2 * half // CHUNKS, LANES), BF16),
            pltpu.VMEM((CHUNKS, 2 * half // CHUNKS, LANES), BF16),
            pltpu.VMEM((4, CAP, BLK, features), BF16),
            pltpu.VMEM((4 * CAP + 1, BLK, features), BF16),
            pltpu.VMEM((rows, features), F32),
            pltpu.VMEM((rows, 2 * features), BF16),
            dma((messages,)),
            dma((messages,)),
            dma((4, most)),
            dma((4, most)),
            dma((4, PIECES)),
            dma((4, PIECES)),
        ],
        compiler_params=pltpu.CompilerParams(
            collective_id=1, has_side_effects=True, vmem_limit_bytes=30 << 20
        ),
        name="exchange",
    )(
        table,
        grads,
        shipped,
        context,
        d_query,
        w_query_key,
        w_value,
        w_out,
        sorted_rows,
        order,
        gain,
        gain_part,
    )

    shape = jax.ShapeDtypeStruct
    grad_qk, grad_value, grad_out, grad_gain, branch, grad_tokens = pl.pallas_call(
        finish_kernel,
        out_shape=[
            shape((features, 2 * features), F32),
            shape((features, features), F32),
            shape((features, features), F32),
            shape((1, features), F32),
            shape((rows, features), BF16),
            shape((rows, features), F32),
        ],
        in_specs=[ON_CHIP] * 5,
        out_specs=[OFF_CHIP] * 3 + [ON_CHIP] + [OFF_CHIP] * 2,
        scratch_shapes=[
            pltpu.VMEM((features, 2 * features), F32),
            pltpu.VMEM((features, features), F32),
            pltpu.VMEM((features, features), F32),
            dma((5,)),
        ],
        compiler_params=pltpu.CompilerParams(vmem_limit_bytes=24 << 20),
        name="finish",
    )(gathered, gain_sum, gain, branch, grad_tokens)
    return (
        branch[None, None],
        grad_tokens[None, None],
        grad_qk,
        grad_value,
        grad_out,
        grad_gain.reshape(features),
    )


def solution(mesh):
    bricks = P("bx", "by", None, None)
    placed = (bricks, P(), P(), P(), P(), bricks, P("bx", "by", None), P(), P())
    return jax.shard_map(
        shards,
        mesh=mesh,
        in_specs=placed,
        out_specs=(bricks, bricks, P(), P(), P(), P()),
        check_vma=False,
    )
```
